32 devices in a mesh: grp: 4 (over y, x), pos: 8 (over z, core).
Axes of the slice: x: 2, y: 2, z: 4, core: 2. Of those that a mesh axis runs over, the one named last changes fastest.
Arguments:
- tiles: float32 [4, 8, 12, 256, 256], P('grp', 'pos'), may hold values from -0.109375 to 0.109375
- tile_row: int32 [4, 8, 12], P('grp', 'pos'), may hold values from 0 to 7
- tile_col: int32 [4, 8, 12], P('grp', 'pos'), may hold values from 0 to 7
- tile_count: int32 [4, 8], P('grp', 'pos'), may hold values from 1 to 12, as said below
- energies: float32 [16384], P('pos'), may hold values from 1 to 10
- basis: float32 [16, 16384], P(None, 'pos'), may hold values from -6 to 6
- prev_basis: float32 [16, 16384], P(None, 'pos'), may hold values from -6 to 6
- beta_prev: float32 [16, 16], replicated, may hold values from -3 to 3
Outputs:
- next_basis: float32 [16, 16384], P(None, 'pos')
- alpha: float32 [16, 16], replicated
- beta: float32 [16, 16], replicated
The draws below stay inside these ranges and needn't reach their ends.
Inputs may be any that keep to these rules, and one draw needn't show every extreme that they name: `tile_count`: some segment of some diagonal uses all 12 slots in every draw.
All inputs are finite; a program needn't handle non-finite values.
Results may differ from the reference program's by a relative error of at most 0.00021.
Values sent between devices are 32-bit elements; how exact they have to be, the bound alone decides.
A program may use at most 64 MiB of HBM per device.

```python
import math
import jax
import jax.numpy as jnp
from jax import lax

TILE = 256
BLOCK = 16
TPS = 8
MAXT = 12
GROUPS = 4
SEGS = 8
NDIM = 16384


def draw_tile_count(key, part):
    first_key, second_key = jax.random.split(jax.random.fold_in(key, 17))
    counts = jax.random.randint(first_key, (GROUPS * SEGS,), 1, MAXT + 1)
    chosen = jax.random.randint(second_key, (), 0, GROUPS * SEGS)
    counts = counts.at[chosen].set(MAXT)
    return counts.reshape(GROUPS, SEGS).astype(jnp.int32)


def with_ends(drawn, rng, least, largest):
    shape = drawn.shape
    index_at = [jax.random.randint(jax.random.fold_in(rng, axis), (), 0, shape[axis]) for axis in range(len(shape))]
    drawn = drawn.at[tuple(index_at)].set(least)
    longest = shape.index(max(shape))
    index_at[longest] = (index_at[longest] + 1) % shape[longest]
    return drawn.at[tuple(index_at)].set(largest)


def steps_of(own_key, extent, pieces, least, high):
    def one(position, blocks):
        steps = jax.random.uniform(jax.random.fold_in(jax.random.fold_in(own_key, 6), position), (blocks,), jnp.float32, least / len(pieces), high / len(pieces))
        return jnp.repeat(jnp.exp(steps), extent[position] // blocks).reshape((-1,) + (1,) * (len(extent) - position - 1))

    gain = one(*pieces[0])
    for cut in pieces[1:]:
        gain = gain * one(*cut)
    return gain


def bell_draw(key, dims, deviation, most, shards=(), kind=jnp.bfloat16):
    entries = deviation * jax.random.normal(key, dims, jnp.float32)
    if shards:
        entries = entries * steps_of(key, dims, shards, -0.22, 0.18)
    return jnp.clip(entries, -most, most).astype(kind)


def setup_inputs(seed: int = 0) -> dict:
    key_of = jax.random.split(jax.random.key(seed), 9)
    tiles = bell_draw(key_of[0], (GROUPS, SEGS, MAXT, TILE, TILE), (2 * TILE * MAXT * GROUPS // TPS) ** -0.5, 0.109375, ((0, 4), (1, 8)), jnp.float32)
    tile_row = with_ends(jax.random.randint(key_of[1], (GROUPS, SEGS, MAXT), 0, TPS), jax.random.fold_in(key_of[1], 1), 0, TPS - 1).astype(jnp.int32)
    tile_col = with_ends(jax.random.randint(key_of[2], (GROUPS, SEGS, MAXT), 0, TPS), jax.random.fold_in(key_of[2], 1), 0, TPS - 1).astype(jnp.int32)
    tile_count = draw_tile_count(jax.random.fold_in(key_of[8], 71), 0)
    energies = jnp.clip(jnp.exp(math.log(10.0) - 2.3025851 * jax.random.uniform(key_of[4], (NDIM,), jnp.float32) ** steps_of(key_of[4], (NDIM,), ((0, 8),), -0.2, 0.2)), 1.0, 10.0)
    basis = bell_draw(key_of[5], (BLOCK, NDIM), 1.0, 6.0, ((1, 8),), jnp.float32)
    prev_basis = bell_draw(key_of[6], (BLOCK, NDIM), 1.0, 6.0, ((1, 8),), jnp.float32)
    beta_prev = bell_draw(key_of[7], (BLOCK, BLOCK), 0.5, 3.0, (), jnp.float32)
    return {"tiles": tiles, "tile_row": tile_row, "tile_col": tile_col, "tile_count": tile_count, "energies": energies, "basis": basis, "prev_basis": prev_basis, "beta_prev": beta_prev}


def matmul(left, right):
    return jnp.dot(left, right, precision=lax.Precision.HIGHEST)

def reference(tiles, tile_row, tile_col, tile_count, energies, basis, prev_basis, beta_prev):
    group_ids = jnp.arange(GROUPS, dtype=jnp.int32)[:, None, None]
    pos_ids = jnp.arange(SEGS, dtype=jnp.int32)[None, :, None]
    slot_ids = jnp.arange(MAXT, dtype=jnp.int32)[None, None, :]
    row_start = ((pos_ids * TPS + tile_row) * TILE).astype(jnp.int32).reshape(-1)
    col_start = (((pos_ids + group_ids) % SEGS * TPS + tile_col) * TILE).astype(jnp.int32).reshape(-1)
    weight_on = (slot_ids < tile_count[:, :, None]).astype(jnp.float32).reshape(-1)
    block_data = tiles.reshape(-1, TILE, TILE)

    def advance(accumulated, entry):
        data, row_at, col_at, scale = entry
        from_col = lax.dynamic_slice_in_dim(basis, col_at, TILE, 1)
        from_row = lax.dynamic_slice_in_dim(basis, row_at, TILE, 1)
        to_row = matmul(from_col, data.T) * scale
        to_col = matmul(from_row, data) * scale
        current = lax.dynamic_slice_in_dim(accumulated, row_at, TILE, 1)
        accumulated = lax.dynamic_update_slice_in_dim(accumulated, current + to_row, row_at, 1)
        current = lax.dynamic_slice_in_dim(accumulated, col_at, TILE, 1)
        accumulated = lax.dynamic_update_slice_in_dim(accumulated, current + to_col, col_at, 1)
        return (accumulated, None)
    applied, unused = lax.scan(advance, jnp.zeros_like(basis), (block_data, row_start, col_start, weight_on))
    applied = applied + energies[None, :] * basis
    alpha = matmul(basis, applied.T) / NDIM
    residual = applied - matmul(alpha.T, basis) - matmul(beta_prev, prev_basis)
    gram = matmul(residual, residual.T) / NDIM
    factor = jnp.linalg.cholesky(gram)
    next_rows = jax.scipy.linalg.solve_triangular(factor, residual, lower=True)
    return (next_rows, alpha, factor)
```

```python
import functools

import jax
import jax.numpy as jnp
from jax import lax
from jax.experimental import pallas as pl
from jax.experimental.pallas import tpu as pltpu
from jax.sharding import PartitionSpec as P

MESH = pl.DeviceIdType.MESH
NT = (((1,), (1,)), ((), ()))
NN = (((1,), (0,)), ((), ()))
f32 = jnp.float32
bf16 = jnp.bfloat16
CORES = 2
TERMS = ((0, 0), (0, 1), (1, 0), (0, 2), (2, 0), (1, 1))


def exact(left, right, dims):
    return lax.dot_general(
        left, right, dims, precision=lax.Precision.HIGHEST, preferred_element_type=f32
    )


def split(values):
    high = values.astype(bf16)
    return high, (values - high.astype(f32)).astype(bf16)


def split3(values):
    high = values.astype(bf16)
    rest = values - high.astype(f32)
    middle = rest.astype(bf16)
    return high, middle, (rest - middle.astype(f32)).astype(bf16)


def packed(values):
    half = values.shape[0] // 2
    return jnp.concatenate([values[:half], values[half:]], axis=1)


def unpacked(values):
    half = values.shape[1] // 2
    return jnp.concatenate([values[:, :half], values[:, half:]], axis=0)


def sources(group, length):
    half, quarter = length // 2, length // 4
    low, high = group & (group - 1), group - (1 << (group.bit_length() - 1))
    if low == high:
        return [(group, 0, half), (low, half, half)]
    return [(group, 0, half), (low, half, quarter), (high, half + quarter, quarter)]


def factored(gram, extra):
    n = gram.shape[0]
    wide = jnp.concatenate([extra, gram], axis=1)
    width = wide.shape[1]
    row_at = lax.broadcasted_iota(jnp.int32, (n, 1), 0)
    columns = [jnp.broadcast_to(gram[:, k : k + 1], (n, width)) for k in range(n)]
    done = jnp.zeros((n, width), f32)
    for j in range(n):
        corner = columns[j][j : j + 1]
        inverse = 1.0 / corner
        row = wide[j : j + 1]
        done = jnp.where(row_at == j, row * lax.rsqrt(corner), done)
        for k in range(j + 1, n):
            columns[k] = columns[k] - columns[j] * (columns[k][j : j + 1] * inverse)
        wide = wide - columns[j] * (row * inverse)
    return done[:, : width - n], done[:, width - n :]


def kernel(
    groups, segs,
    tiles_hbm, row_hbm, col_hbm, count_hbm, energies_hbm, basis_hbm, prev_hbm, beta_prev_hbm,
    stack_ref, sums_ref,
    tiles, highs, lows, rows, cols, count, energies, own, far, prev, beta_prev,
    own_split, far_split, products, back, forth, arrived, rest, near, late,
    in_sem, tile_sem, far_send, far_recv, back_send, back_recv, forth_send, forth_recv,
    gather_send, gather_recv, near_send, near_recv, late_send, late_recv,
):
    g, p = lax.axis_index("grp"), lax.axis_index("pos")
    slots, width = tiles.shape[0], tiles.shape[-1]
    vectors, length = own.shape
    sides = length // width
    part = length // groups
    chips = segs // CORES
    core, chip = lax.rem(p, CORES), p // CORES
    step = next(n for n in (4, 3, 2, 1) if slots % n == 0)

    def at(group, pos):
        return (group, lax.rem(pos + segs, segs))

    def partner(d):
        other, bit = g, 1
        while bit < groups:
            if d & bit:
                other = other + bit - 2 * bit * lax.rem(g // bit, 2)
            bit *= 2
        return other

    def send(src, dst, send_sem, recv_sem, to):
        return pltpu.make_async_remote_copy(
            src_ref=src, dst_ref=dst, send_sem=send_sem, recv_sem=recv_sem,
            device_id=to, device_id_type=MESH,
        )

    mates = [(d, c) for d in reversed(range(groups)) for c in range(CORES) if d or c]

    def mate(d, c):
        return (partner(d), p + c * (1 - 2 * core))

    barrier = pltpu.get_barrier_semaphore()

    def greet(to):
        pl.semaphore_signal(barrier, inc=1, device_id=to, device_id_type=MESH)

    greeted = [0] * groups
    for mine in range(1, groups):
        for source, _, _ in sources(mine, length):
            greeted[source] += 1

        @pl.when(g == mine)
        def _():
            for source, _, _ in sources(mine, length):
                greet(at(source, p + mine))

    for d in range(1, chips):
        greet(at(g, p + CORES * d))
    for d, c in mates:
        greet(mate(d, c))
    for d in range(1, groups):
        greet(at(partner(d), p - partner(d) + segs))

    @pl.when(g != 0)
    def _():
        greet(at(g, p - g + segs))

    small = [
        pltpu.make_async_copy(src, dst, in_sem.at[i])
        for i, (src, dst) in enumerate([
            (basis_hbm, own), (prev_hbm, prev), (energies_hbm, energies),
            (beta_prev_hbm, beta_prev), (row_hbm, rows), (col_hbm, cols), (count_hbm, count),
        ])
    ]
    for copy in small:
        copy.start()

    def tile_copy(k):
        return pltpu.make_async_copy(tiles_hbm.at[k], tiles.at[k], tile_sem.at[k])

    for k in range(slots):
        tile_copy(k).start()

    def stack(ref, out):
        for t in range(sides):
            high, low = split(ref[:, t * width : (t + 1) * width])
            out[t] = jnp.concatenate([high, low], axis=0)

    def multiply(picked, high, low, dims):
        both_parts = lax.dot_general(picked, high, dims, preferred_element_type=f32)
        both_parts += lax.dot_general(picked, low, dims, preferred_element_type=f32)
        return both_parts[:vectors] + both_parts[vectors:]

    def scatter(index, out):
        for t in range(sides):
            value = jnp.zeros((vectors, width), f32)
            for k in range(slots):
                live = jnp.logical_and(index[0, k] == t, k < count[0, 0])
                value = value + products[k] * jnp.where(live, 1.0, 0.0).astype(f32)
            cut = min(width, part)
            for c in range(0, width, cut):
                lane = t * width + c
                out[lane // part, :, lane % part : lane % part + cut] = value[:, c : c + cut]

    with jax.named_scope("ph_barrier"):
        for mine in range(groups):
            expected = greeted[mine] + (chips - 1) + len(mates) + (groups - 1) + (1 if mine else 0)

            @pl.when(g == mine)
            def _():
                pl.semaphore_wait(barrier, expected)

    def far_copy(to_group, i):
        _, first, lanes = sources(to_group, length)[i]
        lanes = slice(first, first + lanes)
        return send(
            basis_hbm.at[:, lanes], far.at[:, lanes], far_send.at[to_group], far_recv.at[i],
            at(to_group, p - to_group + segs),
        )

    far_copies = [
        (source, to_group, i)
        for to_group in reversed(range(1, groups))
        for i, (source, _, _) in enumerate(sources(to_group, length))
    ]
    for source, to_group, i in far_copies:
        pl.when(g == source)(far_copy(to_group, i).start)

    with jax.named_scope("ph_small"):
        for copy in small:
            copy.wait()

    @pl.when(g == 0)
    def _():
        far[...] = own[...]

    stack(own, own_split)

    def backward(i, carry):
        for j in range(step):
            tile_copy(i * step + j).wait()
        for j in range(step):
            k = i * step + j
            high, low = split(tiles[k])
            highs[k], lows[k] = high, low
            products[k] = multiply(own_split[rows[0, k]], high, low, NN)
        return carry

    with jax.named_scope("ph_bwd"):
        lax.fori_loop(0, slots // step, backward, 0)
    with jax.named_scope("ph_scat1"):
        scatter(cols, back)

    back_copies = [
        send(back.at[partner(d)], arrived.at[d], back_send.at[d], back_recv.at[d], at(partner(d), p + g))
        for d in range(groups)
    ]
    for copy in reversed(back_copies[1:]):
        copy.start()

    @pl.when(g != 0)
    def _():
        back_copies[0].start()

    @pl.when(g == 0)
    def _():
        arrived[0] = back[g]

    with jax.named_scope("ph_pre"):
        lanes = pl.ds(pl.multiple_of(g * part, part), part)
        basis_part, prev_part = own[:, lanes], prev[:, lanes]
        own_own = exact(basis_part, basis_part, NT)
        shift = exact(beta_prev[...], exact(prev_part, basis_part, NT), NN)
        offset = energies[:, lanes] * basis_part - exact(beta_prev[...], prev_part, NN)

    with jax.named_scope("ph_farwait"):
        for mine in range(1, groups):
            @pl.when(g == mine)
            def _():
                for i in range(len(sources(mine, length))):
                    far_copy(mine, i).wait_recv()

    stack(far, far_split)

    def forward(i, carry):
        for j in range(step):
            k = i * step + j
            products[k] = multiply(far_split[cols[0, k]], highs[k], lows[k], NT)
        return carry

    with jax.named_scope("ph_fwd"):
        lax.fori_loop(0, slots // step, forward, 0)
    with jax.named_scope("ph_scat2"):
        scatter(rows, forth)

    forth_copies = [
        send(
            forth.at[partner(d)], arrived.at[groups + d - 1], forth_send.at[d], forth_recv.at[d],
            at(partner(d), p),
        )
        for d in range(1, groups)
    ]
    for copy in reversed(forth_copies):
        copy.start()
    with jax.named_scope("ph_kown"):
        pieces = split3(own[...])
        for i, (_, piece) in enumerate(TERMS):
            stack_ref[(2 * i + 1) * vectors : (2 * i + 2) * vectors, :] = pieces[piece]
    with jax.named_scope("ph_rswait"):
        for copy in forth_copies + back_copies[1:]:
            copy.wait_recv()
        pl.when(g != 0)(back_copies[0].wait_recv)

    with jax.named_scope("ph_gram"):
        mine = forth[g] + offset
        for d in range(2 * groups - 1):
            mine = mine + arrived[d]
        rest[:, lanes] = mine
        rest_own, rest_rest = exact(mine, basis_part, NT), exact(mine, mine, NT)
        slot = g * CORES + core
        near[slot] = packed(
            jnp.concatenate([own_own, rest_own + shift, rest_own, rest_rest], axis=1)
        )
    near_copies = [
        send(near.at[slot], near.at[slot], near_send.at[i], near_recv.at[i], mate(d, c))
        for i, (d, c) in enumerate(mates)
    ]
    for copy in near_copies:
        copy.start()
    gather_copies = [
        send(rest.at[:, lanes], rest.at[:, lanes], gather_send.at[d], gather_recv.at[d], at(partner(d), p))
        for d in range(1, groups)
    ]
    for copy in reversed(gather_copies):
        copy.start()
    with jax.named_scope("ph_nearwait"):
        for copy in near_copies:
            copy.wait_recv()
    total = near[0]
    for i in range(1, groups * CORES):
        total = total + near[i]
    late[chip] = total
    late_copies = [
        send(late.at[chip], late.at[chip], late_send.at[d], late_recv.at[d], at(g, p + CORES * d))
        for d in range(1, chips)
    ]
    for copy in reversed(late_copies):
        copy.start()
    with jax.named_scope("ph_gatherwait"):
        for copy in gather_copies:
            copy.wait_recv()
    with jax.named_scope("ph_krest"):
        pieces = split3(rest[...])
        for i, (_, piece) in enumerate(TERMS):
            stack_ref[2 * i * vectors : (2 * i + 1) * vectors, :] = pieces[piece]

    with jax.named_scope("ph_sendwait"):
        for copy in forth_copies + back_copies[1:] + gather_copies + near_copies:
            copy.wait_send()
        pl.when(g != 0)(back_copies[0].wait_send)
        for source, to_group, i in far_copies:
            pl.when(g == source)(far_copy(to_group, i).wait_send)
    with jax.named_scope("ph_latewait"):
        for copy in late_copies:
            copy.wait()
    total = late[0]
    for i in range(1, chips):
        total = total + late[i]
    sums_ref[...] = total


def finish(total, sums_ref, stack_ref, next_ref, alpha_ref, beta_ref):
    vectors = next_ref.shape[0]
    sums = unpacked(sums_ref[...])
    own_own, applied_own, rest_own, rest_rest = (
        sums[:, i * vectors : (i + 1) * vectors] for i in range(4)
    )
    alpha_t = applied_own / total
    alpha_ref[...] = alpha_t.T
    gram = (
        rest_rest
        + exact(exact(alpha_t, own_own, NN) - rest_own, alpha_t, NT)
        - exact(alpha_t, rest_own, NT)
    ) / total
    row_at = lax.broadcasted_iota(jnp.int32, (vectors, vectors), 0)
    col_at = lax.broadcasted_iota(jnp.int32, (vectors, vectors), 1)
    identity = jnp.where(row_at == col_at, 1.0, 0.0).astype(f32)
    with jax.named_scope("ph_factor"):
        weights, upper = factored(gram, jnp.concatenate([identity, -alpha_t], axis=1))
    beta_ref[...] = upper.T
    pieces = split3(weights)
    left = jnp.concatenate([pieces[piece] for piece, _ in TERMS], axis=1)
    with jax.named_scope("ph_last"):
        next_ref[...] = lax.dot_general(left, stack_ref[...], NN, preferred_element_type=f32)


def shards(groups, segs, tiles, tile_row, tile_col, tile_count, energies, basis, prev_basis, beta_prev):
    slots, width = tiles.shape[2], tiles.shape[-1]
    vectors, length = basis.shape
    sides, part, chips = length // width, length // groups, segs // CORES
    dma = pltpu.SemaphoreType.DMA
    block = (vectors, length)
    message = (vectors // 2, 8 * vectors)
    vmem = pl.BlockSpec(memory_space=pltpu.VMEM)
    stack, sums = pl.pallas_call(
        functools.partial(kernel, groups, segs),
        out_shape=(
            pltpu.VMEM((2 * len(TERMS) * vectors, length), bf16),
            pltpu.VMEM(message, f32),
        ),
        in_specs=[pl.BlockSpec(memory_space=pltpu.HBM)] * 8,
        out_specs=(vmem, vmem),
        scratch_shapes=[
            pltpu.VMEM((slots, width, width), f32),
            pltpu.VMEM((slots, width, width), bf16),
            pltpu.VMEM((slots, width, width), bf16),
            pltpu.SMEM((1, slots), jnp.int32),
            pltpu.SMEM((1, slots), jnp.int32),
            pltpu.SMEM((1, 1), jnp.int32),
            pltpu.VMEM((1, length), f32),
            pltpu.VMEM(block, f32),
            pltpu.VMEM(block, f32),
            pltpu.VMEM(block, f32),
            pltpu.VMEM((vectors, vectors), f32),
            pltpu.VMEM((sides, 2 * vectors, width), bf16),
            pltpu.VMEM((sides, 2 * vectors, width), bf16),
            pltpu.VMEM((slots, vectors, width), f32),
            pltpu.VMEM((groups, vectors, part), f32),
            pltpu.VMEM((groups, vectors, part), f32),
            pltpu.VMEM((2 * groups - 1, vectors, part), f32),
            pltpu.VMEM(block, f32),
            pltpu.VMEM((groups * CORES, *message), f32),
            pltpu.VMEM((chips, *message), f32),
            dma((7,)), dma((slots,)), dma((groups,)), dma((3,)),
            dma((groups,)), dma((groups,)), dma((groups,)), dma((groups,)),
            dma((groups,)), dma((groups,)),
            dma((groups * CORES,)), dma((groups * CORES,)), dma((chips,)), dma((chips,)),
        ],
        compiler_params=pltpu.CompilerParams(collective_id=0, has_side_effects=True),
    )(
        tiles.reshape(slots, width, width),
        tile_row.reshape(1, slots),
        tile_col.reshape(1, slots),
        tile_count.reshape(1, 1),
        energies.reshape(1, length),
        basis,
        prev_basis,
        beta_prev,
    )
    return pl.pallas_call(
        functools.partial(finish, float(length * segs)),
        out_shape=(
            jax.ShapeDtypeStruct(block, f32),
            jax.ShapeDtypeStruct((vectors, vectors), f32),
            jax.ShapeDtypeStruct((vectors, vectors), f32),
        ),
        in_specs=[vmem, vmem],
        out_specs=(vmem, vmem, vmem),
    )(
        pltpu.with_memory_space_constraint(sums, pltpu.VMEM),
        pltpu.with_memory_space_constraint(stack, pltpu.VMEM),
    )


def solution(mesh):
    groups, segs = mesh.shape["grp"], mesh.shape["pos"]
    in_specs = (
        P("grp", "pos", None, None, None),
        P("grp", "pos", None),
        P("grp", "pos", None),
        P("grp", "pos"),
        P("pos"),
        P(None, "pos"),
        P(None, "pos"),
        P(),
    )
    out_specs = (P(None, "pos"), P(), P())
    return jax.shard_map(
        functools.partial(shards, groups, segs),
        mesh=mesh, in_specs=in_specs, out_specs=out_specs, check_vma=False,
    )
```

```python
import functools

import jax
import jax.numpy as jnp
from jax import lax
from jax.experimental import pallas as pl
from jax.experimental.pallas import tpu as pltpu
from jax.sharding import PartitionSpec as P

MESH = pl.DeviceIdType.MESH
NT = (((1,), (1,)), ((), ()))
NN = (((1,), (0,)), ((), ()))
f32 = jnp.float32
bf16 = jnp.bfloat16
CORES = 2
LANES = 128
TERMS = ((0, 0), (0, 1), (1, 0), (0, 2), (2, 0), (1, 1))


def exact(left, right, dims):
    return lax.dot_general(
        left, right, dims, precision=lax.Precision.HIGHEST, preferred_element_type=f32
    )


def split(values):
    high = values.astype(bf16)
    return high, (values - high.astype(f32)).astype(bf16)


def split3(values):
    high = values.astype(bf16)
    rest = values - high.astype(f32)
    middle = rest.astype(bf16)
    return high, middle, (rest - middle.astype(f32)).astype(bf16)


def packed(values):
    rows = values.shape[0] // 8
    return jnp.concatenate([values[i * rows : (i + 1) * rows] for i in range(8)], axis=1)


def unpacked(values):
    lanes = values.shape[1] // 8
    return jnp.concatenate([values[:, i * lanes : (i + 1) * lanes] for i in range(8)], axis=0)


def folded(values):
    rows = values.size // LANES
    return jnp.concatenate([values[i : i + rows] for i in range(0, values.shape[0], rows)], axis=1)


def unfolded(values, lanes):
    return jnp.concatenate([values[:, i : i + lanes] for i in range(0, LANES, lanes)], axis=0)


def sources(group, length):
    half, quarter = length // 2, length // 4
    low, high = group & (group - 1), group - (1 << (group.bit_length() - 1))
    if low == high:
        return [(group, 0, half), (low, half, half)]
    return [(group, 0, half), (low, half, quarter), (high, half + quarter, quarter)]


def factored(gram, extra):
    n = gram.shape[0]
    wide = jnp.concatenate([extra, gram], axis=1)
    width = wide.shape[1]
    row_at = lax.broadcasted_iota(jnp.int32, (n, 1), 0)
    columns = [jnp.broadcast_to(gram[:, k : k + 1], (n, width)) for k in range(n)]
    done = jnp.zeros((n, width), f32)
    for j in range(n):
        corner = columns[j][j : j + 1]
        inverse = 1.0 / corner
        row = wide[j : j + 1]
        done = jnp.where(row_at == j, row * lax.rsqrt(corner), done)
        for k in range(j + 1, n):
            columns[k] = columns[k] - columns[j] * (columns[k][j : j + 1] * inverse)
        wide = wide - columns[j] * (row * inverse)
    return done[:, : width - n], done[:, width - n :]


def flipped(value, d, count):
    out, bit = value, 1
    while bit < count:
        if not isinstance(d, int) or d & bit:
            out = out + (d // bit % 2) * (bit - 2 * bit * lax.rem(value // bit, 2))
        bit *= 2
    return out


def kernel(
    groups, segs, total,
    tiles_hbm, row_hbm, col_hbm, count_hbm, energies_hbm, basis_hbm, prev_hbm, beta_prev_hbm,
    stack_ref, alpha_ref, known_ref, sums_ref,
    tiles, highs, lows, rows, cols, count, energies, own, far, prev, beta_prev,
    own_split, far_split, products, back, relay, forth, arrived, rest, near, late, mids, lasts,
    in_sem, tile_sem, far_send, far_recv, sent, came, ready,
):
    g, p = lax.axis_index("grp"), lax.axis_index("pos")
    slots, width = tiles.shape[0], tiles.shape[-1]
    vectors, length = own.shape
    sides = length // width
    part = length // groups
    chips, devices = segs // CORES, groups * segs
    core, chip = lax.rem(p, CORES), p // CORES
    step = slots // tile_sem.shape[0]
    others = groups - 1
    CROSS, BACK, FORTH, GATHER, NEAR, LATE, MIDS, LASTS = range(8)

    def at(group, pos):
        return (group, lax.rem(pos + segs, segs))

    def partner(d):
        return flipped(g, d, groups)

    def send(src, dst, send_sem, recv_sem, to):
        return pltpu.make_async_remote_copy(
            src_ref=src, dst_ref=dst, send_sem=send_sem, recv_sem=recv_sem,
            device_id=to, device_id_type=MESH,
        )

    def post(which, src, dst, to):
        return send(src, dst, sent.at[which], came.at[which], to)

    def landed(which, ref):
        pltpu.make_async_copy(ref, ref, came.at[which]).wait()

    def gone(which, ref):
        pltpu.make_async_copy(ref, ref, sent.at[which]).wait()

    mates = [(d, c) for d in reversed(range(groups)) for c in range(CORES) if d or c]

    def mate(d, c):
        return (partner(d), flipped(p, c, CORES))

    barrier = pltpu.get_barrier_semaphore()

    def greet(to):
        pl.semaphore_signal(barrier, inc=1, device_id=to, device_id_type=MESH)

    greeted = [0] * groups
    for mine in range(1, groups):
        for source, _, _ in sources(mine, length):
            greeted[source] += 1

        @pl.when(g == mine)
        def _():
            for source, _, _ in sources(mine, length):
                greet(at(source, p + mine))

    column = sorted({CORES * d for d in range(1, chips)} | {segs - d for d in range(1, groups)})
    for d in column:
        greet(at(g, p + d))
    for d, c in mates:
        greet(mate(d, c))

    small = [
        pltpu.make_async_copy(src, dst, in_sem.at[i])
        for i, (src, dst) in enumerate([
            (basis_hbm, own), (row_hbm, rows), (col_hbm, cols), (count_hbm, count),
            (prev_hbm, prev), (energies_hbm, energies), (beta_prev_hbm, beta_prev),
        ])
    ]
    for copy in small:
        copy.start()

    def tile_copy(i):
        some = pl.ds(i * step, step)
        return pltpu.make_async_copy(tiles_hbm.at[some], tiles.at[some], tile_sem.at[i])

    for i in range(slots // step):
        tile_copy(i).start()

    def stack(ref, out):
        for t in range(sides):
            high, low = split(ref[:, t * width : (t + 1) * width])
            out[t] = jnp.concatenate([high, low], axis=0)

    def multiply(picked, high, low, dims):
        both_parts = lax.dot_general(picked, high, dims, preferred_element_type=f32)
        both_parts += lax.dot_general(picked, low, dims, preferred_element_type=f32)
        return both_parts[:vectors] + both_parts[vectors:]

    def scatter(index, out):
        for t in range(sides):
            value = jnp.zeros((vectors, width), f32)
            for k in range(slots):
                live = jnp.logical_and(index[0, k] == t, k < count[0, 0])
                value = value + products[k] * jnp.where(live, 1.0, 0.0).astype(f32)
            cut = min(width, part)
            for c in range(0, width, cut):
                lane = t * width + c
                out[lane // part, :, lane % part : lane % part + cut] = value[:, c : c + cut]

    def far_copy(to_group, i):
        _, first, lanes = sources(to_group, length)[i]
        lanes = slice(first, first + lanes)
        return send(
            basis_hbm.at[:, lanes], far.at[:, lanes], far_send.at[to_group], far_recv.at[i],
            at(to_group, p - to_group + segs),
        )

    far_copies = [
        (source, to_group, i)
        for to_group in reversed(range(1, groups))
        for i, (source, _, _) in enumerate(sources(to_group, length))
    ]

    def backward():
        with jax.named_scope("ph_small"):
            for copy in small:
                copy.wait()
        stack(own, own_split)

        def some(i, carry):
            tile_copy(i).wait()
            for j in range(step):
                k = i * step + j
                high, low = split(tiles[k])
                highs[k], lows[k] = high, low
                products[k] = multiply(own_split[rows[0, k]], high, low, NN)
            return carry

        with jax.named_scope("ph_bwd"):
            lax.fori_loop(0, slots // step, some, 0)
        scatter(cols, back)

    early = p < segs // 2
    pl.when(early)(backward)
    with jax.named_scope("ph_barrier"):
        for mine in range(groups):
            @pl.when(g == mine)
            def _():
                pl.semaphore_wait(barrier, greeted[mine] + len(column) + len(mates))
    for source, to_group, i in far_copies:
        pl.when(g == source)(far_copy(to_group, i).start)
    for d in range(1, chips):
        pl.semaphore_signal(ready, inc=1, device_id=at(g, p + CORES * d), device_id_type=MESH)
    pl.when(jnp.logical_not(early))(backward)

    for d in reversed(range(1, groups)):
        post(CROSS, back.at[partner(d)], relay.at[d], at(partner(d), p)).start()

    @pl.when(g == 0)
    def _():
        far[...] = own[...]

    with jax.named_scope("ph_pre"):
        lanes = pl.ds(pl.multiple_of(g * part, part), part)
        basis_part, prev_part = own[:, lanes], prev[:, lanes]
        weighted = energies[:, lanes] * basis_part
        both = jnp.concatenate([basis_part, weighted, prev_part], axis=0)
        inner = exact(both, basis_part, NT)
        inner = jnp.concatenate(
            [
                inner[: 2 * vectors],
                exact(beta_prev[...], inner[2 * vectors :], NN),
                jnp.zeros((vectors, vectors), f32),
            ],
            axis=0,
        )
        offset = weighted - exact(beta_prev[...], prev_part, NN)
        slot = g * CORES + core
        near[slot] = packed(inner)
    for d, c in mates:
        post(NEAR, near.at[slot], near.at[slot], mate(d, c)).start()

    def relay_on():
        pl.when(g != 0)(post(BACK, back.at[g], arrived.at[0], at(g, p + g)).start)
        with jax.named_scope("ph_cross"):
            landed(CROSS, relay.at[pl.ds(1, others)])
        for d in reversed(range(1, groups)):
            pl.when(g != d)(post(BACK, relay.at[d], arrived.at[d], at(g, p + partner(d))).start)
        for d in range(groups):
            @pl.when(g == d)
            def _():
                arrived[d] = relay[d] if d else back[0]

    last_chip = p >= segs - CORES
    pl.when(jnp.logical_not(last_chip))(relay_on)

    with jax.named_scope("ph_farwait"):
        for mine in range(1, groups):
            @pl.when(g == mine)
            def _():
                for i in range(len(sources(mine, length))):
                    far_copy(mine, i).wait_recv()

    stack(far, far_split)

    def forward(i, carry):
        for j in range(step):
            k = i * step + j
            products[k] = multiply(far_split[cols[0, k]], highs[k], lows[k], NT)
        return carry

    with jax.named_scope("ph_fwd"):
        lax.fori_loop(0, slots // step, forward, 0)
    with jax.named_scope("ph_scat2"):
        scatter(rows, forth)

    for d in reversed(range(1, groups)):
        post(FORTH, forth.at[partner(d)], arrived.at[groups + d - 1], at(partner(d), p)).start()
    pl.when(last_chip)(relay_on)

    def to_all(which, buffer, value):
        me = g * segs + p
        buffer[me] = value

        def copy(dg, dp):
            return post(which, buffer.at[me], buffer.at[me], (flipped(g, dg, groups), flipped(p, dp, segs)))

        if devices <= 64:
            apart = [(dp, dg) for dp in reversed(range(segs)) for dg in reversed(range(groups))]
            for dp, dg in apart[:-1]:
                copy(dg, dp).start()
        else:
            def one(d, carry):
                copy(d // segs, lax.rem(d, segs)).start()
                return carry

            lax.fori_loop(1, devices, one, 0)

    def summed(buffer):
        value = buffer[0]
        for i in range(1, buffer.shape[0]):
            value = value + buffer[i]
        return value

    with jax.named_scope("ph_mid"):
        mid = jnp.zeros((vectors, vectors), f32)
        for h in range(groups):
            mid = mid + exact(back[h], far[:, h * part : (h + 1) * part], NT)
        pl.semaphore_wait(ready, chips - 1)
        to_all(MIDS, mids, folded(mid + mid.T))

    with jax.named_scope("ph_near"):
        landed(NEAR, near.at[pl.ds(0, groups * CORES - 1)])
        late[chip] = summed(near)
    for d in reversed(range(1, chips)):
        post(LATE, late.at[chip], late.at[chip], at(g, p + CORES * d)).start()

    with jax.named_scope("ph_kown"):
        pieces = split3(own[...])
        for i, (_, piece) in enumerate(TERMS):
            stack_ref[(2 * i + 1) * vectors : (2 * i + 2) * vectors, :] = pieces[piece]
    with jax.named_scope("ph_rswait"):
        landed(BACK, arrived.at[pl.ds(0, others)])
        landed(FORTH, arrived.at[pl.ds(groups, others)])

    with jax.named_scope("ph_gram"):
        mine = forth[g] + offset
        for d in range(2 * groups - 1):
            mine = mine + arrived[d]
        rest[:, lanes] = mine
        to_all(LASTS, lasts, folded(exact(mine, mine, NT)))
    for d in reversed(range(1, groups)):
        post(GATHER, rest.at[:, lanes], rest.at[:, lanes], at(partner(d), p)).start()

    with jax.named_scope("ph_latewait"):
        landed(LATE, late.at[pl.ds(0, chips - 1)])
    with jax.named_scope("ph_gatherwait"):
        landed(GATHER, rest.at[:, pl.ds(0, others * part)])
    with jax.named_scope("ph_krest"):
        pieces = split3(rest[...])
        for i, (_, piece) in enumerate(TERMS):
            stack_ref[2 * i * vectors : (2 * i + 1) * vectors, :] = pieces[piece]
    with jax.named_scope("ph_sendwait"):
        gone(CROSS, back.at[pl.ds(0, others)])
        gone(BACK, relay.at[pl.ds(0, others)])
        gone(FORTH, forth.at[pl.ds(0, others)])
        gone(GATHER, rest.at[:, pl.ds(0, others * part)])
        gone(NEAR, near.at[pl.ds(0, groups * CORES - 1)])
        gone(LATE, late.at[pl.ds(0, chips - 1)])
        gone(MIDS, mids.at[pl.ds(0, devices - 1)])
        gone(LASTS, lasts.at[pl.ds(0, devices - 1)])
        for source, to_group, i in far_copies:
            pl.when(g == source)(far_copy(to_group, i).wait_send)
    with jax.named_scope("ph_midswait"):
        landed(MIDS, mids.at[pl.ds(0, devices - 1)])
    with jax.named_scope("ph_known"):
        inner = unpacked(summed(late))
        own_own, shift = inner[:vectors], inner[2 * vectors : 3 * vectors]
        applied_own = inner[vectors : 2 * vectors] + unfolded(summed(mids), vectors)
        rest_own, alpha_t = applied_own - shift, applied_own / total
        alpha_ref[...] = alpha_t
        known_ref[...] = (
            exact(exact(alpha_t, own_own, NN) - rest_own, alpha_t, NT) - exact(alpha_t, rest_own, NT)
        )
    with jax.named_scope("ph_lastswait"):
        landed(LASTS, lasts.at[pl.ds(0, devices - 1)])
    sums_ref[...] = summed(lasts)


def finish(total, sums_ref, alpha_t_ref, known_ref, stack_ref, next_ref, alpha_ref, beta_ref):
    vectors = next_ref.shape[0]
    alpha_t = alpha_t_ref[...]
    alpha_ref[...] = alpha_t.T
    gram = (unfolded(sums_ref[...], vectors) + known_ref[...]) / total
    row_at = lax.broadcasted_iota(jnp.int32, (vectors, vectors), 0)
    col_at = lax.broadcasted_iota(jnp.int32, (vectors, vectors), 1)
    identity = jnp.where(row_at == col_at, 1.0, 0.0).astype(f32)
    with jax.named_scope("ph_factor"):
        weights, upper = factored(gram, jnp.concatenate([identity, -alpha_t], axis=1))
    beta_ref[...] = upper.T
    pieces = split3(weights)
    left = jnp.concatenate([pieces[piece] for piece, _ in TERMS], axis=1)
    with jax.named_scope("ph_last"):
        next_ref[...] = lax.dot_general(left, stack_ref[...], NN, preferred_element_type=f32)


def shards(groups, segs, tiles, tile_row, tile_col, tile_count, energies, basis, prev_basis, beta_prev):
    slots, width = tiles.shape[2], tiles.shape[-1]
    vectors, length = basis.shape
    sides, part, chips = length // width, length // groups, segs // CORES
    step = next(n for n in (4, 3, 2, 1) if slots % n == 0)
    total = float(length * segs)
    dma = pltpu.SemaphoreType.DMA
    block, square = (vectors, length), (vectors, vectors)
    message, fold = (vectors // 2, 8 * vectors), (vectors * vectors // LANES, LANES)
    vmem = pl.BlockSpec(memory_space=pltpu.VMEM)
    stack, alpha_t, known, sums = pl.pallas_call(
        functools.partial(kernel, groups, segs, total),
        out_shape=(
            pltpu.VMEM((2 * len(TERMS) * vectors, length), bf16),
            pltpu.VMEM(square, f32),
            pltpu.VMEM(square, f32),
            pltpu.VMEM(fold, f32),
        ),
        in_specs=[pl.BlockSpec(memory_space=pltpu.HBM)] * 8,
        out_specs=(vmem,) * 4,
        scratch_shapes=[
            pltpu.VMEM((slots, width, width), f32),
            pltpu.VMEM((slots, width, width), bf16),
            pltpu.VMEM((slots, width, width), bf16),
            pltpu.SMEM((1, slots), jnp.int32),
            pltpu.SMEM((1, slots), jnp.int32),
            pltpu.SMEM((1, 1), jnp.int32),
            pltpu.VMEM((1, length), f32),
            pltpu.VMEM(block, f32),
            pltpu.VMEM(block, f32),
            pltpu.VMEM(block, f32),
            pltpu.VMEM(square, f32),
            pltpu.VMEM((sides, 2 * vectors, width), bf16),
            pltpu.VMEM((sides, 2 * vectors, width), bf16),
            pltpu.VMEM((slots, vectors, width), f32),
            pltpu.VMEM((groups, vectors, part), f32),
            pltpu.VMEM((groups, vectors, part), f32),
            pltpu.VMEM((groups, vectors, part), f32),
            pltpu.VMEM((2 * groups - 1, vectors, part), f32),
            pltpu.VMEM(block, f32),
            pltpu.VMEM((groups * CORES, *message), f32),
            pltpu.VMEM((chips, *message), f32),
            pltpu.VMEM((groups * segs, *fold), f32),
            pltpu.VMEM((groups * segs, *fold), f32),
            dma((7,)), dma((slots // step,)), dma((groups,)), dma((3,)), dma((8,)), dma((8,)),
            pltpu.SemaphoreType.REGULAR,
        ],
        compiler_params=pltpu.CompilerParams(collective_id=0, has_side_effects=True),
    )(
        tiles.reshape(slots, width, width),
        tile_row.reshape(1, slots),
        tile_col.reshape(1, slots),
        tile_count.reshape(1, 1),
        energies.reshape(1, length),
        basis,
        prev_basis,
        beta_prev,
    )
    held = [pltpu.with_memory_space_constraint(x, pltpu.VMEM) for x in (sums, alpha_t, known, stack)]
    return pl.pallas_call(
        functools.partial(finish, total),
        out_shape=(
            jax.ShapeDtypeStruct(block, f32),
            jax.ShapeDtypeStruct(square, f32),
            jax.ShapeDtypeStruct(square, f32),
        ),
        in_specs=[vmem] * 4,
        out_specs=(vmem, vmem, vmem),
    )(*held)


def solution(mesh):
    groups, segs = mesh.shape["grp"], mesh.shape["pos"]
    in_specs = (
        P("grp", "pos", None, None, None),
        P("grp", "pos", None),
        P("grp", "pos", None),
        P("grp", "pos"),
        P("pos"),
        P(None, "pos"),
        P(None, "pos"),
        P(),
    )
    out_specs = (P(None, "pos"), P(), P())
    return jax.shard_map(
        functools.partial(shards, groups, segs),
        mesh=mesh, in_specs=in_specs, out_specs=out_specs, check_vma=False,
    )
```

```python
import functools

import jax
import jax.numpy as jnp
from jax import lax
from jax.experimental import pallas as pl
from jax.experimental.pallas import tpu as pltpu
from jax.sharding import PartitionSpec as P

MESH = pl.DeviceIdType.MESH
NT = (((1,), (1,)), ((), ()))
NN = (((1,), (0,)), ((), ()))
f32 = jnp.float32
bf16 = jnp.bfloat16
CORES = 2
LANES = 128
TERMS = ((0, 0), (0, 1), (1, 0), (0, 2), (2, 0), (1, 1))


def exact(left, right, dims):
    return lax.dot_general(
        left, right, dims, precision=lax.Precision.HIGHEST, preferred_element_type=f32
    )


def split(values):
    high = values.astype(bf16)
    return high, (values - high.astype(f32)).astype(bf16)


def split3(values):
    high = values.astype(bf16)
    rest = values - high.astype(f32)
    middle = rest.astype(bf16)
    return high, middle, (rest - middle.astype(f32)).astype(bf16)


def packed(values):
    rows = values.shape[0] // 8
    return jnp.concatenate([values[i * rows : (i + 1) * rows] for i in range(8)], axis=1)


def unpacked(values):
    lanes = values.shape[1] // 8
    return jnp.concatenate([values[:, i * lanes : (i + 1) * lanes] for i in range(8)], axis=0)


def folded(values):
    rows = values.size // LANES
    return jnp.concatenate([values[i : i + rows] for i in range(0, values.shape[0], rows)], axis=1)


def unfolded(values, lanes):
    return jnp.concatenate([values[:, i : i + lanes] for i in range(0, LANES, lanes)], axis=0)


def sources(group, length):
    half, quarter = length // 2, length // 4
    low, high = group & (group - 1), group - (1 << (group.bit_length() - 1))
    if low == high:
        own = half + quarter if group == 1 else half
        return [(group, 0, own), (low, own, length - own)]
    return [(group, 0, half), (low, half, quarter), (high, half + quarter, quarter)]


def factored(gram, extra):
    n = gram.shape[0]
    wide = jnp.concatenate([extra, gram], axis=1)
    width = wide.shape[1]
    row_at = lax.broadcasted_iota(jnp.int32, (n, 1), 0)
    columns = [jnp.broadcast_to(gram[:, k : k + 1], (n, width)) for k in range(n)]
    done = jnp.zeros((n, width), f32)
    for j in range(n):
        corner = columns[j][j : j + 1]
        inverse = 1.0 / corner
        row = wide[j : j + 1]
        done = jnp.where(row_at == j, row * lax.rsqrt(corner), done)
        for k in range(j + 1, n):
            columns[k] = columns[k] - columns[j] * (columns[k][j : j + 1] * inverse)
        wide = wide - columns[j] * (row * inverse)
    return done[:, : width - n], done[:, width - n :]


def flipped(value, d, count):
    out, bit = value, 1
    while bit < count:
        if not isinstance(d, int) or d & bit:
            out = out + (d // bit % 2) * (bit - 2 * bit * lax.rem(value // bit, 2))
        bit *= 2
    return out


def kernel(
    groups, segs, total,
    tiles_hbm, row_hbm, col_hbm, count_hbm, energies_hbm, basis_hbm, prev_hbm, beta_prev_hbm,
    stack_ref, alpha_ref, known_ref, sums_ref,
    tiles, highs, lows, rows, cols, count, energies, own, far, prev, beta_prev,
    own_split, far_split, products, back, relay, forth, arrived, rest, near, late, mids, lasts,
    in_sem, tile_sem, far_send, far_recv, sent, came, ready,
):
    g, p = lax.axis_index("grp"), lax.axis_index("pos")
    slots, width = tiles.shape[0], tiles.shape[-1]
    vectors, length = own.shape
    sides = length // width
    part = length // groups
    chips, devices = segs // CORES, groups * segs
    core, chip = lax.rem(p, CORES), p // CORES
    step = slots // tile_sem.shape[0]
    others = groups - 1
    CROSS, BACK, FORTH, GATHER, NEAR, LATE, MIDS, LASTS = range(8)

    def at(group, pos):
        return (group, lax.rem(pos + segs, segs))

    def partner(d):
        return flipped(g, d, groups)

    def send(src, dst, send_sem, recv_sem, to):
        return pltpu.make_async_remote_copy(
            src_ref=src, dst_ref=dst, send_sem=send_sem, recv_sem=recv_sem,
            device_id=to, device_id_type=MESH,
        )

    def post(which, src, dst, to):
        return send(src, dst, sent.at[which], came.at[which], to)

    def landed(which, ref):
        pltpu.make_async_copy(ref, ref, came.at[which]).wait()

    def gone(which, ref):
        pltpu.make_async_copy(ref, ref, sent.at[which]).wait()

    def settle_back(sems):
        whole = jnp.logical_and(p >= segs - CORES, g != 0)
        for count_of, yes in ((groups, whole), (others, jnp.logical_not(whole))):
            ref = arrived.at[pl.ds(0, count_of)]
            pl.when(yes)(pltpu.make_async_copy(ref, ref, sems.at[BACK]).wait)

    mates = [(d, c) for d in reversed(range(groups)) for c in range(CORES) if d or c]

    def mate(d, c):
        return (partner(d), flipped(p, c, CORES))

    barrier = pltpu.get_barrier_semaphore()

    def greet(to):
        pl.semaphore_signal(barrier, inc=1, device_id=to, device_id_type=MESH)

    greeted = [0] * groups
    for mine in range(1, groups):
        for source, _, _ in sources(mine, length):
            greeted[source] += 1

        @pl.when(g == mine)
        def _():
            for source, _, _ in sources(mine, length):
                greet(at(source, p + mine))

    last_chip = p >= segs - CORES

    def of_last_chip(pos):
        return lax.rem(pos + segs, segs) >= segs - CORES

    for d in range(1, groups):
        @pl.when(jnp.logical_and(g != d, of_last_chip(p - d)))
        def _():
            greet(at(d, p - d))

    column = sorted({CORES * d for d in range(1, chips)} | {segs - d for d in range(1, groups)})
    for d in column:
        greet(at(g, p + d))
    for d, c in mates:
        greet(mate(d, c))

    small = [
        pltpu.make_async_copy(src, dst, in_sem.at[i])
        for i, (src, dst) in enumerate([
            (basis_hbm, own), (row_hbm, rows), (col_hbm, cols), (count_hbm, count),
            (prev_hbm, prev), (energies_hbm, energies), (beta_prev_hbm, beta_prev),
        ])
    ]
    for copy in small:
        copy.start()

    def tile_copy(i):
        some = pl.ds(i * step, step)
        return pltpu.make_async_copy(tiles_hbm.at[some], tiles.at[some], tile_sem.at[i])

    for i in range(slots // step):
        tile_copy(i).start()

    def stack(ref, out):
        for t in range(sides):
            high, low = split(ref[:, t * width : (t + 1) * width])
            out[t] = jnp.concatenate([high, low], axis=0)

    def multiply(picked, high, low, dims):
        both_parts = lax.dot_general(picked, high, dims, preferred_element_type=f32)
        both_parts += lax.dot_general(picked, low, dims, preferred_element_type=f32)
        return both_parts[:vectors] + both_parts[vectors:]

    def added(index, t):
        value = jnp.zeros((vectors, width), f32)
        for k in range(slots):
            live = jnp.logical_and(index[0, k] == t, k < count[0, 0])
            value = value + products[k] * jnp.where(live, 1.0, 0.0).astype(f32)
        return value

    def scatter(index, out, then=lambda d: None):
        whole = part // width
        for d in reversed(range(groups)):
            for t in range(whole):
                h = partner(d)
                out[h, :, t * width : (t + 1) * width] = added(index, h * whole + t)
            if whole:
                then(d)
        if not whole:
            for t in range(sides):
                value = added(index, t)
                for c in range(0, width, part):
                    out[(t * width + c) // part] = value[:, c : c + part]
            for d in reversed(range(groups)):
                then(d)

    def far_copy(to_group, i):
        _, first, lanes = sources(to_group, length)[i]
        lanes = slice(first, first + lanes)
        return send(
            own.at[:, lanes], far.at[:, lanes], far_send.at[to_group], far_recv.at[i],
            at(to_group, p - to_group + segs),
        )

    far_copies = [
        (source, to_group, i)
        for to_group in reversed(range(1, groups))
        for i, (source, _, _) in enumerate(sources(to_group, length))
    ]

    def backward():
        with jax.named_scope("ph_small"):
            for copy in small[1:4]:
                copy.wait()
        stack(own, own_split)

        def some(i, carry):
            tile_copy(i).wait()
            for j in range(step):
                k = i * step + j
                high, low = split(tiles[k])
                highs[k], lows[k] = high, low
                products[k] = multiply(own_split[rows[0, k]], high, low, NN)
            return carry

        with jax.named_scope("ph_bwd"):
            lax.fori_loop(0, slots // step, some, 0)
        scatter(cols, back)

    early = p < segs // 2
    small[0].wait()
    pl.when(early)(backward)
    with jax.named_scope("ph_barrier"):
        for mine in range(groups):
            expected = greeted[mine] + len(column) + len(mates)
            for last in (True, False):
                @pl.when(jnp.logical_and(g == mine, last_chip == last))
                def _():
                    pl.semaphore_wait(barrier, expected + (others if last and mine else 0))

    for last in (True, False):
        for source, to_group, i in far_copies:
            turn = of_last_chip(p - to_group) == last
            pl.when(jnp.logical_and(g == source, turn))(far_copy(to_group, i).start)
    for d in range(1, chips):
        pl.semaphore_signal(ready, inc=1, device_id=at(g, p + CORES * d), device_id_type=MESH)
    pl.when(jnp.logical_not(early))(backward)

    @pl.when(jnp.logical_not(last_chip))
    def _():
        for d in reversed(range(1, groups)):
            post(CROSS, back.at[partner(d)], relay.at[d], at(partner(d), p)).start()

    @pl.when(g == 0)
    def _():
        far[...] = own[...]

    with jax.named_scope("ph_pre"):
        for copy in small[4:]:
            copy.wait()
        lanes = pl.ds(pl.multiple_of(g * part, part), part)
        basis_part, prev_part = own[:, lanes], prev[:, lanes]
        weighted = energies[:, lanes] * basis_part
        both = jnp.concatenate([basis_part, weighted, prev_part], axis=0)
        inner = exact(both, basis_part, NT)
        inner = jnp.concatenate(
            [
                inner[: 2 * vectors],
                exact(beta_prev[...], inner[2 * vectors :], NN),
                jnp.zeros((vectors, vectors), f32),
            ],
            axis=0,
        )
        offset = weighted - exact(beta_prev[...], prev_part, NN)
        slot = g * CORES + core
        near[slot] = packed(inner)
    for d, c in mates:
        post(NEAR, near.at[slot], near.at[slot], mate(d, c)).start()

    @pl.when(last_chip)
    def _():
        for d in reversed(range(groups)):
            @pl.when(jnp.logical_or(g != 0, d != 0))
            def _():
                post(BACK, back.at[partner(d)], arrived.at[d], at(partner(d), p + g)).start()

        @pl.when(g == 0)
        def _():
            arrived[0] = back[0]

    def relay_on():
        with jax.named_scope("ph_cross"):
            landed(CROSS, relay.at[pl.ds(1, others)])
        for d in reversed(range(1, groups)):
            pl.when(g != d)(post(BACK, relay.at[d], arrived.at[d], at(g, p + partner(d))).start)
        pl.when(g != 0)(post(BACK, back.at[g], arrived.at[0], at(g, p + g)).start)
        for d in range(groups):
            @pl.when(g == d)
            def _():
                arrived[d] = relay[d] if d else back[0]

    pl.when(early)(relay_on)

    with jax.named_scope("ph_farwait"):
        for mine in range(1, groups):
            @pl.when(g == mine)
            def _():
                for i in range(len(sources(mine, length))):
                    far_copy(mine, i).wait_recv()

    stack(far, far_split)

    with jax.named_scope("ph_fwd"):
        for k in range(slots):
            products[k] = multiply(far_split[cols[0, k]], highs[k], lows[k], NT)
    with jax.named_scope("ph_scat2"):
        def pass_on(d):
            if d:
                post(FORTH, forth.at[partner(d)], arrived.at[groups + d - 1], at(partner(d), p)).start()

        scatter(rows, forth, pass_on)
    pl.when(jnp.logical_not(jnp.logical_or(early, last_chip)))(relay_on)

    def to_all(which, buffer, value):
        me = g * segs + p
        buffer[me] = value

        def copy(dg, dp):
            return post(which, buffer.at[me], buffer.at[me], (flipped(g, dg, groups), flipped(p, dp, segs)))

        if devices <= 64:
            apart = [
                (dp * CORES + c, dg)
                for dp in reversed(range(chips)) for dg in reversed(range(groups)) for c in range(CORES)
            ]
            apart.remove((0, 0))
            for dp, dg in apart:
                copy(dg, dp).start()
        else:
            def one(d, carry):
                copy(d // segs, lax.rem(d, segs)).start()
                return carry

            lax.fori_loop(1, devices, one, 0)

    def summed(buffer):
        value = buffer[0]
        for i in range(1, buffer.shape[0]):
            value = value + buffer[i]
        return value

    with jax.named_scope("ph_mid"):
        mid = jnp.zeros((vectors, vectors), f32)
        for h in range(groups):
            mid = mid + exact(back[h], far[:, h * part : (h + 1) * part], NT)
        pl.semaphore_wait(ready, chips - 1)
        to_all(MIDS, mids, folded(mid + mid.T))

    with jax.named_scope("ph_near"):
        landed(NEAR, near.at[pl.ds(0, groups * CORES - 1)])
        late[chip] = summed(near)
    for d in reversed(range(1, chips)):
        post(LATE, late.at[chip], late.at[chip], at(g, p + CORES * d)).start()

    with jax.named_scope("ph_kown"):
        pieces = split3(own[...])
        for i, (_, piece) in enumerate(TERMS):
            stack_ref[(2 * i + 1) * vectors : (2 * i + 2) * vectors, :] = pieces[piece]
    with jax.named_scope("ph_rswait"):
        settle_back(came)
        landed(FORTH, arrived.at[pl.ds(groups, others)])

    with jax.named_scope("ph_gram"):
        mine = forth[g] + offset
        for d in range(2 * groups - 1):
            mine = mine + arrived[d]
        rest[:, lanes] = mine
        value = folded(exact(mine, mine, NT))
        for d in reversed(range(1, groups)):
            post(GATHER, rest.at[:, lanes], rest.at[:, lanes], at(partner(d), p)).start()
        to_all(LASTS, lasts, value)

    with jax.named_scope("ph_latewait"):
        landed(LATE, late.at[pl.ds(0, chips - 1)])
    with jax.named_scope("ph_gatherwait"):
        landed(GATHER, rest.at[:, pl.ds(0, others * part)])
    with jax.named_scope("ph_krest"):
        pieces = split3(rest[...])
        for i, (_, piece) in enumerate(TERMS):
            stack_ref[2 * i * vectors : (2 * i + 1) * vectors, :] = pieces[piece]
    with jax.named_scope("ph_sendwait"):
        pl.when(jnp.logical_not(last_chip))(lambda: gone(CROSS, back.at[pl.ds(0, others)]))
        settle_back(sent)
        gone(FORTH, forth.at[pl.ds(0, others)])
        gone(GATHER, rest.at[:, pl.ds(0, others * part)])
        gone(NEAR, near.at[pl.ds(0, groups * CORES - 1)])
        gone(LATE, late.at[pl.ds(0, chips - 1)])
        gone(MIDS, mids.at[pl.ds(0, devices - 1)])
        gone(LASTS, lasts.at[pl.ds(0, devices - 1)])
        for source, to_group, i in far_copies:
            pl.when(g == source)(far_copy(to_group, i).wait_send)
    with jax.named_scope("ph_midswait"):
        landed(MIDS, mids.at[pl.ds(0, devices - 1)])
    with jax.named_scope("ph_known"):
        inner = unpacked(summed(late))
        own_own, shift = inner[:vectors], inner[2 * vectors : 3 * vectors]
        applied_own = inner[vectors : 2 * vectors] + unfolded(summed(mids), vectors)
        rest_own, alpha_t = applied_own - shift, applied_own / total
        alpha_ref[...] = alpha_t
        known_ref[...] = (
            exact(exact(alpha_t, own_own, NN) - rest_own, alpha_t, NT) - exact(alpha_t, rest_own, NT)
        )
    with jax.named_scope("ph_lastswait"):
        landed(LASTS, lasts.at[pl.ds(0, devices - 1)])
    sums_ref[...] = summed(lasts)


def finish(total, sums_ref, alpha_t_ref, known_ref, stack_ref, next_ref, alpha_ref, beta_ref):
    vectors = next_ref.shape[0]
    alpha_t = alpha_t_ref[...]
    alpha_ref[...] = alpha_t.T
    gram = (unfolded(sums_ref[...], vectors) + known_ref[...]) / total
    row_at = lax.broadcasted_iota(jnp.int32, (vectors, vectors), 0)
    col_at = lax.broadcasted_iota(jnp.int32, (vectors, vectors), 1)
    identity = jnp.where(row_at == col_at, 1.0, 0.0).astype(f32)
    with jax.named_scope("ph_factor"):
        weights, upper = factored(gram, jnp.concatenate([identity, -alpha_t], axis=1))
    beta_ref[...] = upper.T
    pieces = split3(weights)
    left = jnp.concatenate([pieces[piece] for piece, _ in TERMS], axis=1)
    with jax.named_scope("ph_last"):
        next_ref[...] = lax.dot_general(left, stack_ref[...], NN, preferred_element_type=f32)


def shards(groups, segs, tiles, tile_row, tile_col, tile_count, energies, basis, prev_basis, beta_prev):
    slots, width = tiles.shape[2], tiles.shape[-1]
    vectors, length = basis.shape
    sides, part, chips = length // width, length // groups, segs // CORES
    step = next(n for n in (4, 3, 2, 1) if slots % n == 0)
    total = float(length * segs)
    dma = pltpu.SemaphoreType.DMA
    block, square = (vectors, length), (vectors, vectors)
    message, fold = (vectors // 2, 8 * vectors), (vectors * vectors // LANES, LANES)
    vmem = pl.BlockSpec(memory_space=pltpu.VMEM)
    stack, alpha_t, known, sums = pl.pallas_call(
        functools.partial(kernel, groups, segs, total),
        out_shape=(
            pltpu.VMEM((2 * len(TERMS) * vectors, length), bf16),
            pltpu.VMEM(square, f32),
            pltpu.VMEM(square, f32),
            pltpu.VMEM(fold, f32),
        ),
        in_specs=[pl.BlockSpec(memory_space=pltpu.HBM)] * 8,
        out_specs=(vmem,) * 4,
        scratch_shapes=[
            pltpu.VMEM((slots, width, width), f32),
            pltpu.VMEM((slots, width, width), bf16),
            pltpu.VMEM((slots, width, width), bf16),
            pltpu.SMEM((1, slots), jnp.int32),
            pltpu.SMEM((1, slots), jnp.int32),
            pltpu.SMEM((1, 1), jnp.int32),
            pltpu.VMEM((1, length), f32),
            pltpu.VMEM(block, f32),
            pltpu.VMEM(block, f32),
            pltpu.VMEM(block, f32),
            pltpu.VMEM(square, f32),
            pltpu.VMEM((sides, 2 * vectors, width), bf16),
            pltpu.VMEM((sides, 2 * vectors, width), bf16),
            pltpu.VMEM((slots, vectors, width), f32),
            pltpu.VMEM((groups, vectors, part), f32),
            pltpu.VMEM((groups, vectors, part), f32),
            pltpu.VMEM((groups, vectors, part), f32),
            pltpu.VMEM((2 * groups - 1, vectors, part), f32),
            pltpu.VMEM(block, f32),
            pltpu.VMEM((groups * CORES, *message), f32),
            pltpu.VMEM((chips, *message), f32),
            pltpu.VMEM((groups * segs, *fold), f32),
            pltpu.VMEM((groups * segs, *fold), f32),
            dma((7,)), dma((slots // step,)), dma((groups,)), dma((3,)), dma((8,)), dma((8,)),
            pltpu.SemaphoreType.REGULAR,
        ],
        compiler_params=pltpu.CompilerParams(collective_id=0, has_side_effects=True),
    )(
        tiles.reshape(slots, width, width),
        tile_row.reshape(1, slots),
        tile_col.reshape(1, slots),
        tile_count.reshape(1, 1),
        energies.reshape(1, length),
        basis,
        prev_basis,
        beta_prev,
    )
    held = [pltpu.with_memory_space_constraint(x, pltpu.VMEM) for x in (sums, alpha_t, known, stack)]
    return pl.pallas_call(
        functools.partial(finish, total),
        out_shape=(
            jax.ShapeDtypeStruct(block, f32),
            jax.ShapeDtypeStruct(square, f32),
            jax.ShapeDtypeStruct(square, f32),
        ),
        in_specs=[vmem] * 4,
        out_specs=(vmem, vmem, vmem),
    )(*held)


def solution(mesh):
    groups, segs = mesh.shape["grp"], mesh.shape["pos"]
    in_specs = (
        P("grp", "pos", None, None, None),
        P("grp", "pos", None),
        P("grp", "pos", None),
        P("grp", "pos"),
        P("pos"),
        P(None, "pos"),
        P(None, "pos"),
        P(),
    )
    out_specs = (P(None, "pos"), P(), P())
    return jax.shard_map(
        functools.partial(shards, groups, segs),
        mesh=mesh, in_specs=in_specs, out_specs=out_specs, check_vma=False,
    )
```

```python
import functools

import jax
import jax.numpy as jnp
from jax import lax
from jax.experimental import pallas as pl
from jax.experimental.pallas import tpu as pltpu
from jax.sharding import PartitionSpec as P

MESH = pl.DeviceIdType.MESH
NT = (((1,), (1,)), ((), ()))
NN = (((1,), (0,)), ((), ()))
f32 = jnp.float32
bf16 = jnp.bfloat16
CORES = 2
LANES = 128
TERMS = ((0, 0), (0, 1), (1, 0), (0, 2), (2, 0), (1, 1))


def exact(left, right, dims):
    return lax.dot_general(
        left, right, dims, precision=lax.Precision.HIGHEST, preferred_element_type=f32
    )


def split(values):
    high = values.astype(bf16)
    return high, (values - high.astype(f32)).astype(bf16)


def split3(values):
    high = values.astype(bf16)
    rest = values - high.astype(f32)
    middle = rest.astype(bf16)
    return high, middle, (rest - middle.astype(f32)).astype(bf16)


def packed(values):
    rows = values.shape[0] // 8
    return jnp.concatenate([values[i * rows : (i + 1) * rows] for i in range(8)], axis=1)


def unpacked(values):
    lanes = values.shape[1] // 8
    return jnp.concatenate([values[:, i * lanes : (i + 1) * lanes] for i in range(8)], axis=0)


def folded(values):
    rows = values.size // LANES
    return jnp.concatenate([values[i : i + rows] for i in range(0, values.shape[0], rows)], axis=1)


def unfolded(values, lanes):
    return jnp.concatenate([values[:, i : i + lanes] for i in range(0, LANES, lanes)], axis=0)


def sources(group, length):
    half, quarter = length // 2, length // 4
    low, high = group & (group - 1), group - (1 << (group.bit_length() - 1))
    if low == high:
        own = half + quarter if group == 1 else half
        return [(group, 0, own), (low, own, length - own)]
    return [(group, 0, half), (low, half, quarter), (high, half + quarter, quarter)]


def factored(gram, wide):
    n = gram.shape[0]
    wide = [*wide, gram]
    row_at = lax.broadcasted_iota(jnp.int32, (n, 1), 0)
    columns = [jnp.broadcast_to(gram[:, k : k + 1], (n, LANES)) for k in range(n)]
    done = [jnp.zeros(x.shape, f32) for x in wide]
    for j in range(n):
        corner = columns[j][j : j + 1]
        inverse, root = 1.0 / corner, lax.rsqrt(corner)
        for i, x in enumerate(wide):
            lanes = x.shape[1]
            row = x[j : j + 1]
            done[i] = jnp.where(row_at == j, row * root[:, :lanes], done[i])
            wide[i] = x - columns[j][:, :lanes] * (row * inverse[:, :lanes])
        for k in range(j + 1, n):
            columns[k] = columns[k] - columns[j] * (columns[k][j : j + 1] * inverse)
    return done[-1], done[:-1]


def flipped(value, d, count):
    out, bit = value, 1
    while bit < count:
        if not isinstance(d, int) or d & bit:
            out = out + (d // bit % 2) * (bit - 2 * bit * lax.rem(value // bit, 2))
        bit *= 2
    return out


def sent_kib(groups, segs, vectors, length, mine, last):
    others, block = groups - 1, vectors * length // groups // 256
    lanes = sum(
        n for to_group in range(1, groups)
        for source, _, n in sources(to_group, length) if source == mine
    )
    blocks = (0 if last else others) + (groups if last and mine else others) + 2 * others
    messages = groups * CORES - 1 + segs // CORES - 1
    return (
        lanes * vectors // 256 + blocks * block
        + (messages * 4 * vectors + 2 * (groups * segs - 1) * vectors) * vectors // 256
    )


def kernel(
    groups, segs, total,
    tiles_hbm, row_hbm, col_hbm, count_hbm, energies_hbm, basis_hbm, prev_hbm, beta_prev_hbm,
    stack_ref, alpha_ref, known_ref, wide_ref, sums_ref,
    tiles, highs, lows, rows, cols, count, energies, own, far, prev, beta_prev,
    own_split, far_split, products, back, relay, forth, arrived, rest, near, late, mids, lasts,
    bulk, in_sem, tile_sem, sent, came, ready,
):
    g, p = lax.axis_index("grp"), lax.axis_index("pos")
    slots, width = tiles.shape[0], tiles.shape[-1]
    vectors, length = own.shape
    sides = length // width
    part = length // groups
    chips, devices = segs // CORES, groups * segs
    core, chip = lax.rem(p, CORES), p // CORES
    step = slots // tile_sem.shape[0]
    others = groups - 1
    FAR, CROSS, BACK, FORTH, GATHER, NEAR, LATE, MIDS, LASTS = range(9)

    def at(group, pos):
        return (group, lax.rem(pos + segs, segs))

    def partner(d):
        return flipped(g, d, groups)

    def send(src, dst, send_sem, recv_sem, to):
        return pltpu.make_async_remote_copy(
            src_ref=src, dst_ref=dst, send_sem=send_sem, recv_sem=recv_sem,
            device_id=to, device_id_type=MESH,
        )

    def post(which, src, dst, to):
        return send(src, dst, sent, came.at[which], to)

    def landed(which, ref):
        pltpu.make_async_copy(ref, ref, came.at[which]).wait()

    def all_gone(mine, last):
        ref = bulk.at[pl.ds(0, sent_kib(groups, segs, vectors, length, mine, last))]
        pltpu.make_async_copy(ref, ref, sent).wait()

    def settle_back():
        whole = jnp.logical_and(p >= segs - CORES, g != 0)
        pl.when(whole)(lambda: landed(BACK, arrived.at[pl.ds(0, groups)]))
        pl.when(jnp.logical_not(whole))(lambda: landed(BACK, arrived.at[pl.ds(0, others)]))

    mates = [(d, c) for d in reversed(range(groups)) for c in range(CORES) if d or c]

    def mate(d, c):
        return (partner(d), flipped(p, c, CORES))

    barrier = pltpu.get_barrier_semaphore()

    def greet(to):
        pl.semaphore_signal(barrier, inc=1, device_id=to, device_id_type=MESH)

    greeted = [0] * groups
    for mine in range(1, groups):
        for source, _, _ in sources(mine, length):
            greeted[source] += 1

        @pl.when(g == mine)
        def _():
            for source, _, _ in sources(mine, length):
                greet(at(source, p + mine))

    last_chip = p >= segs - CORES

    def of_last_chip(pos):
        return lax.rem(pos + segs, segs) >= segs - CORES

    for d in range(1, groups):
        @pl.when(jnp.logical_and(g != d, of_last_chip(p - d)))
        def _():
            greet(at(d, p - d))

    column = sorted({CORES * d for d in range(1, chips)} | {segs - d for d in range(1, groups)})
    for d in column:
        greet(at(g, p + d))
    for d, c in mates:
        greet(mate(d, c))

    small = [
        pltpu.make_async_copy(src, dst, in_sem.at[i])
        for i, (src, dst) in enumerate([
            (basis_hbm, own), (row_hbm, rows), (col_hbm, cols), (count_hbm, count),
            (prev_hbm, prev), (energies_hbm, energies), (beta_prev_hbm, beta_prev),
        ])
    ]
    for copy in small:
        copy.start()

    def tile_copy(i):
        some = pl.ds(i * step, step)
        return pltpu.make_async_copy(tiles_hbm.at[some], tiles.at[some], tile_sem.at[i])

    for i in range(slots // step):
        tile_copy(i).start()

    def stack(ref, out):
        for t in range(sides):
            high, low = split(ref[:, t * width : (t + 1) * width])
            out[t] = jnp.concatenate([high, low], axis=0)

    def multiply(picked, high, low, dims):
        both_parts = lax.dot_general(picked, high, dims, preferred_element_type=f32)
        both_parts += lax.dot_general(picked, low, dims, preferred_element_type=f32)
        return both_parts[:vectors] + both_parts[vectors:]

    def added(index, t):
        value = jnp.zeros((vectors, width), f32)
        for k in range(slots):
            live = jnp.logical_and(index[0, k] == t, k < count[0, 0])
            value = value + products[k] * jnp.where(live, 1.0, 0.0).astype(f32)
        return value

    def scatter(index, out, then=lambda d: None):
        whole = part // width
        for d in reversed(range(groups)):
            for t in range(whole):
                h = partner(d)
                out[h, :, t * width : (t + 1) * width] = added(index, h * whole + t)
            if whole:
                then(d)
        if not whole:
            for t in range(sides):
                value = added(index, t)
                for c in range(0, width, part):
                    out[(t * width + c) // part] = value[:, c : c + part]
            for d in reversed(range(groups)):
                then(d)

    def far_copy(to_group, i):
        _, first, lanes = sources(to_group, length)[i]
        lanes = slice(first, first + lanes)
        return post(FAR, own.at[:, lanes], far.at[:, lanes], at(to_group, p - to_group + segs))

    far_copies = [
        (source, to_group, i)
        for to_group in reversed(range(1, groups))
        for i, (source, _, _) in enumerate(sources(to_group, length))
    ]

    def backward():
        with jax.named_scope("ph_small"):
            for copy in small[1:4]:
                copy.wait()
        stack(own, own_split)

        def some(i, carry):
            tile_copy(i).wait()
            for j in range(step):
                k = i * step + j
                high, low = split(tiles[k])
                highs[k], lows[k] = high, low
                products[k] = multiply(own_split[rows[0, k]], high, low, NN)
            return carry

        with jax.named_scope("ph_bwd"):
            lax.fori_loop(0, slots // step, some, 0)
        scatter(cols, back)

    early = p < segs // 2
    small[0].wait()
    pl.when(early)(backward)
    with jax.named_scope("ph_barrier"):
        for mine in range(groups):
            expected = greeted[mine] + len(column) + len(mates)
            for last in (True, False):
                @pl.when(jnp.logical_and(g == mine, last_chip == last))
                def _():
                    pl.semaphore_wait(barrier, expected + (others if last and mine else 0))

    for last in (True, False):
        for source, to_group, i in far_copies:
            turn = of_last_chip(p - to_group) == last
            pl.when(jnp.logical_and(g == source, turn))(far_copy(to_group, i).start)
    for d in range(1, chips):
        pl.semaphore_signal(ready, inc=1, device_id=at(g, p + CORES * d), device_id_type=MESH)
    pl.when(jnp.logical_not(early))(backward)

    @pl.when(jnp.logical_not(last_chip))
    def _():
        for d in reversed(range(1, groups)):
            post(CROSS, back.at[partner(d)], relay.at[d], at(partner(d), p)).start()

    @pl.when(g == 0)
    def _():
        far[...] = own[...]

    with jax.named_scope("ph_pre"):
        for copy in small[4:]:
            copy.wait()
        lanes = pl.ds(pl.multiple_of(g * part, part), part)
        basis_part, prev_part = own[:, lanes], prev[:, lanes]
        weighted = energies[:, lanes] * basis_part
        both = jnp.concatenate([basis_part, weighted, prev_part], axis=0)
        inner = exact(both, basis_part, NT)
        inner = jnp.concatenate(
            [
                inner[: 2 * vectors],
                exact(beta_prev[...], inner[2 * vectors :], NN),
                jnp.zeros((vectors, vectors), f32),
            ],
            axis=0,
        )
        offset = weighted - exact(beta_prev[...], prev_part, NN)
        slot = g * CORES + core
        near[slot] = packed(inner)
    for d, c in mates:
        post(NEAR, near.at[slot], near.at[slot], mate(d, c)).start()

    @pl.when(last_chip)
    def _():
        for d in reversed(range(groups)):
            @pl.when(jnp.logical_or(g != 0, d != 0))
            def _():
                post(BACK, back.at[partner(d)], arrived.at[d], at(partner(d), p + g)).start()

        @pl.when(g == 0)
        def _():
            arrived[0] = back[0]

    def relay_on():
        with jax.named_scope("ph_cross"):
            landed(CROSS, relay.at[pl.ds(1, others)])
        for d in reversed(range(1, groups)):
            pl.when(g != d)(post(BACK, relay.at[d], arrived.at[d], at(g, p + partner(d))).start)
        pl.when(g != 0)(post(BACK, back.at[g], arrived.at[0], at(g, p + g)).start)
        for d in range(groups):
            @pl.when(g == d)
            def _():
                arrived[d] = relay[d] if d else back[0]

    pl.when(early)(relay_on)

    with jax.named_scope("ph_farwait"):
        pl.when(g != 0)(lambda: landed(FAR, far))

    stack(far, far_split)

    with jax.named_scope("ph_fwd"):
        for k in range(slots):
            products[k] = multiply(far_split[cols[0, k]], highs[k], lows[k], NT)
    with jax.named_scope("ph_scat2"):
        def pass_on(d):
            if d:
                post(FORTH, forth.at[partner(d)], arrived.at[groups + d - 1], at(partner(d), p)).start()

        scatter(rows, forth, pass_on)
    pl.when(jnp.logical_not(jnp.logical_or(early, last_chip)))(relay_on)

    def to_all(which, buffer, value):
        me = g * segs + p
        buffer[me] = value

        def copy(dg, dp):
            return post(which, buffer.at[me], buffer.at[me], (flipped(g, dg, groups), flipped(p, dp, segs)))

        if devices <= 64:
            apart = [
                (dp * CORES + c, dg)
                for dp in reversed(range(chips)) for dg in reversed(range(groups)) for c in range(CORES)
            ]
            apart.remove((0, 0))
            for dp, dg in apart:
                copy(dg, dp).start()
        else:
            def one(d, carry):
                copy(d // segs, lax.rem(d, segs)).start()
                return carry

            lax.fori_loop(1, devices, one, 0)

    def summed(buffer):
        value = buffer[0]
        for i in range(1, buffer.shape[0]):
            value = value + buffer[i]
        return value

    with jax.named_scope("ph_mid"):
        mid = jnp.zeros((vectors, vectors), f32)
        for h in range(groups):
            mid = mid + exact(back[h], far[:, h * part : (h + 1) * part], NT)
        pl.semaphore_wait(ready, chips - 1)
        to_all(MIDS, mids, folded(mid + mid.T))

    with jax.named_scope("ph_near"):
        landed(NEAR, near.at[pl.ds(0, groups * CORES - 1)])
        late[chip] = summed(near)
    for d in reversed(range(1, chips)):
        post(LATE, late.at[chip], late.at[chip], at(g, p + CORES * d)).start()

    with jax.named_scope("ph_kown"):
        pieces = split3(own[...])
        for i, (_, piece) in enumerate(TERMS):
            stack_ref[(2 * i + 1) * vectors : (2 * i + 2) * vectors, :] = pieces[piece]
    with jax.named_scope("ph_rswait"):
        settle_back()
        landed(FORTH, arrived.at[pl.ds(groups, others)])

    with jax.named_scope("ph_gram"):
        mine = forth[g] + offset
        for d in range(2 * groups - 1):
            mine = mine + arrived[d]
        rest[:, lanes] = mine
        value = folded(exact(mine, mine, NT))
        for d in reversed(range(1, groups)):
            post(GATHER, rest.at[:, lanes], rest.at[:, lanes], at(partner(d), p)).start()
        to_all(LASTS, lasts, value)

    with jax.named_scope("ph_latewait"):
        landed(LATE, late.at[pl.ds(0, chips - 1)])
    with jax.named_scope("ph_gatherwait"):
        landed(GATHER, rest.at[:, pl.ds(0, others * part)])
    with jax.named_scope("ph_krest"):
        pieces = split3(rest[...])
        for i, (_, piece) in enumerate(TERMS):
            stack_ref[2 * i * vectors : (2 * i + 1) * vectors, :] = pieces[piece]
    with jax.named_scope("ph_sendwait"):
        for mine in range(groups):
            for last in (True, False):
                @pl.when(jnp.logical_and(g == mine, last_chip == last))
                def _():
                    all_gone(mine, last)
    with jax.named_scope("ph_midswait"):
        landed(MIDS, mids.at[pl.ds(0, devices - 1)])
    with jax.named_scope("ph_known"):
        inner = unpacked(summed(late))
        own_own, shift = inner[:vectors], inner[2 * vectors : 3 * vectors]
        applied_own = inner[vectors : 2 * vectors] + unfolded(summed(mids), vectors)
        rest_own, alpha_t = applied_own - shift, applied_own / total
        alpha_ref[...] = alpha_t
        row_at = lax.broadcasted_iota(jnp.int32, (vectors, vectors), 0)
        col_at = lax.broadcasted_iota(jnp.int32, (vectors, vectors), 1)
        identity = jnp.where(row_at == col_at, 1.0, 0.0).astype(f32)
        wide_ref[...] = jnp.concatenate([identity, -alpha_t] * len(TERMS), axis=1)
        known_ref[...] = (
            exact(exact(alpha_t, own_own, NN) - rest_own, alpha_t, NT) - exact(alpha_t, rest_own, NT)
        )
    with jax.named_scope("ph_lastswait"):
        landed(LASTS, lasts.at[pl.ds(0, devices - 1)])
    sums_ref[...] = summed(lasts)


def finish(
    total, sums_ref, alpha_t_ref, known_ref, wide_ref, stack_ref, next_hbm, alpha_hbm, beta_hbm,
    ahead, alpha, beta, sem,
):
    vectors, length = ahead.shape
    alpha[...] = alpha_t_ref[...].T
    outs = [pltpu.make_async_copy(alpha, alpha_hbm, sem.at[0]), pltpu.make_async_copy(beta, beta_hbm, sem.at[1])]
    outs[0].start()
    gram = (unfolded(sums_ref[...], vectors) + known_ref[...]) / total
    cuts = [slice(i, min(i + LANES, wide_ref.shape[1])) for i in range(0, wide_ref.shape[1], LANES)]
    with jax.named_scope("ph_factor"):
        upper, weights = factored(gram, [wide_ref[:, cut] for cut in cuts])
    left = []
    for cut, values in zip(cuts, weights, strict=True):
        pieces = split3(values)
        term = lax.broadcasted_iota(jnp.int32, values.shape, 1) // (2 * vectors) + cut.start // (2 * vectors)
        value = pieces[0].astype(f32)
        for i, (piece, _) in enumerate(TERMS):
            if piece:
                value = jnp.where(term == i, pieces[piece].astype(f32), value)
        left.append(value.astype(bf16))
    left = jnp.concatenate(left, axis=1)
    with jax.named_scope("ph_last"):
        half = length // 2
        for i in range(2):
            lanes = slice(i * half, (i + 1) * half)
            ahead[:, lanes] = lax.dot_general(left, stack_ref[:, lanes], NN, preferred_element_type=f32)
            outs.append(pltpu.make_async_copy(ahead.at[:, lanes], next_hbm.at[:, lanes], sem.at[2 + i]))
            outs[-1].start()
    beta[...] = upper.T
    outs[1].start()
    for copy in outs:
        copy.wait()


def shards(groups, segs, tiles, tile_row, tile_col, tile_count, energies, basis, prev_basis, beta_prev):
    slots, width = tiles.shape[2], tiles.shape[-1]
    vectors, length = basis.shape
    sides, part, chips = length // width, length // groups, segs // CORES
    step = next(n for n in (4, 3, 2, 1) if slots % n == 0)
    total = float(length * segs)
    dma = pltpu.SemaphoreType.DMA
    block, square = (vectors, length), (vectors, vectors)
    message, fold = (vectors // 2, 8 * vectors), (vectors * vectors // LANES, LANES)
    kib = max(
        sent_kib(groups, segs, vectors, length, mine, last)
        for mine in range(groups) for last in (True, False)
    )
    vmem = pl.BlockSpec(memory_space=pltpu.VMEM)
    stack, alpha_t, known, wide, sums = pl.pallas_call(
        functools.partial(kernel, groups, segs, total),
        out_shape=(
            pltpu.VMEM((2 * len(TERMS) * vectors, length), bf16),
            pltpu.VMEM(square, f32),
            pltpu.VMEM(square, f32),
            pltpu.VMEM((vectors, 2 * len(TERMS) * vectors), f32),
            pltpu.VMEM(fold, f32),
        ),
        in_specs=[pl.BlockSpec(memory_space=pltpu.HBM)] * 8,
        out_specs=(vmem,) * 5,
        scratch_shapes=[
            pltpu.VMEM((slots, width, width), f32),
            pltpu.VMEM((slots, width, width), bf16),
            pltpu.VMEM((slots, width, width), bf16),
            pltpu.SMEM((1, slots), jnp.int32),
            pltpu.SMEM((1, slots), jnp.int32),
            pltpu.SMEM((1, 1), jnp.int32),
            pltpu.VMEM((1, length), f32),
            pltpu.VMEM(block, f32),
            pltpu.VMEM(block, f32),
            pltpu.VMEM(block, f32),
            pltpu.VMEM(square, f32),
            pltpu.VMEM((sides, 2 * vectors, width), bf16),
            pltpu.VMEM((sides, 2 * vectors, width), bf16),
            pltpu.VMEM((slots, vectors, width), f32),
            pltpu.VMEM((groups, vectors, part), f32),
            pltpu.VMEM((groups, vectors, part), f32),
            pltpu.VMEM((groups, vectors, part), f32),
            pltpu.VMEM((2 * groups - 1, vectors, part), f32),
            pltpu.VMEM(block, f32),
            pltpu.VMEM((groups * CORES, *message), f32),
            pltpu.VMEM((chips, *message), f32),
            pltpu.VMEM((groups * segs, *fold), f32),
            pltpu.VMEM((groups * segs, *fold), f32),
            pltpu.VMEM((kib, *fold), f32),
            dma((7,)), dma((slots // step,)), dma, dma((9,)),
            pltpu.SemaphoreType.REGULAR,
        ],
        compiler_params=pltpu.CompilerParams(collective_id=0, has_side_effects=True),
    )(
        tiles.reshape(slots, width, width),
        tile_row.reshape(1, slots),
        tile_col.reshape(1, slots),
        tile_count.reshape(1, 1),
        energies.reshape(1, length),
        basis,
        prev_basis,
        beta_prev,
    )
    held = [pltpu.with_memory_space_constraint(x, pltpu.VMEM) for x in (sums, alpha_t, known, wide, stack)]
    return pl.pallas_call(
        functools.partial(finish, total),
        out_shape=(
            jax.ShapeDtypeStruct(block, f32),
            jax.ShapeDtypeStruct(square, f32),
            jax.ShapeDtypeStruct(square, f32),
        ),
        in_specs=[vmem] * 5,
        out_specs=(pl.BlockSpec(memory_space=pltpu.HBM),) * 3,
        scratch_shapes=[pltpu.VMEM(block, f32), pltpu.VMEM(square, f32), pltpu.VMEM(square, f32), dma((4,))],
    )(*held)


def solution(mesh):
    groups, segs = mesh.shape["grp"], mesh.shape["pos"]
    in_specs = (
        P("grp", "pos", None, None, None),
        P("grp", "pos", None),
        P("grp", "pos", None),
        P("grp", "pos"),
        P("pos"),
        P(None, "pos"),
        P(None, "pos"),
        P(),
    )
    out_specs = (P(None, "pos"), P(), P())
    return jax.shard_map(
        functools.partial(shards, groups, segs),
        mesh=mesh, in_specs=in_specs, out_specs=out_specs, check_vma=False,
    )
```

```python
import functools

import jax
import jax.numpy as jnp
from jax import lax
from jax.experimental import pallas as pl
from jax.experimental.pallas import tpu as pltpu
from jax.sharding import PartitionSpec as P

MESH = pl.DeviceIdType.MESH
NT = (((1,), (1,)), ((), ()))
NN = (((1,), (0,)), ((), ()))
f32 = jnp.float32
bf16 = jnp.bfloat16
CORES = 2
LANES = 128
TERMS = ((0, 0), (0, 1), (1, 0), (0, 2), (2, 0), (1, 1))


def exact(left, right, dims):
    return lax.dot_general(
        left, right, dims, precision=lax.Precision.HIGHEST, preferred_element_type=f32
    )


def split(values):
    high = values.astype(bf16)
    return high, (values - high.astype(f32)).astype(bf16)


def split3(values):
    high = values.astype(bf16)
    rest = values - high.astype(f32)
    middle = rest.astype(bf16)
    return high, middle, (rest - middle.astype(f32)).astype(bf16)


def packed(values):
    rows = values.shape[0] // 8
    return jnp.concatenate([values[i * rows : (i + 1) * rows] for i in range(8)], axis=1)


def unpacked(values):
    lanes = values.shape[1] // 8
    return jnp.concatenate([values[:, i * lanes : (i + 1) * lanes] for i in range(8)], axis=0)


def folded(values):
    rows = values.size // LANES
    return jnp.concatenate([values[i : i + rows] for i in range(0, values.shape[0], rows)], axis=1)


def unfolded(values, lanes):
    return jnp.concatenate([values[:, i : i + lanes] for i in range(0, LANES, lanes)], axis=0)


def sources(group, length):
    half, quarter = length // 2, length // 4
    low, high = group & (group - 1), group - (1 << (group.bit_length() - 1))
    if low == high:
        own = half + quarter if group == 1 else half
        return [(group, 0, own), (low, own, length - own)]
    return [(group, 0, half), (low, half, quarter), (high, half + quarter, quarter)]


def factored(gram, wide):
    n = gram.shape[0]
    wide = [*wide, gram]
    row_at = lax.broadcasted_iota(jnp.int32, (n, 1), 0)
    columns = [jnp.broadcast_to(gram[:, k : k + 1], (n, LANES)) for k in range(n)]
    done = [jnp.zeros(x.shape, f32) for x in wide]
    for j in range(n):
        corner = columns[j][j : j + 1]
        inverse, root = 1.0 / corner, lax.rsqrt(corner)
        for i, x in enumerate(wide):
            lanes = x.shape[1]
            row = x[j : j + 1]
            done[i] = jnp.where(row_at == j, row * root[:, :lanes], done[i])
            wide[i] = x - columns[j][:, :lanes] * (row * inverse[:, :lanes])
        for k in range(j + 1, n):
            columns[k] = columns[k] - columns[j] * (columns[k][j : j + 1] * inverse)
    return done[-1], done[:-1]


def flipped(value, d, count):
    out, bit = value, 1
    while bit < count:
        if not isinstance(d, int) or d & bit:
            out = out + (d // bit % 2) * (bit - 2 * bit * lax.rem(value // bit, 2))
        bit *= 2
    return out


def sent_kib(groups, segs, vectors, length, mine, last):
    others, block = groups - 1, vectors * length // groups // 256
    lanes = sum(
        n for to_group in range(1, groups)
        for source, _, n in sources(to_group, length) if source == mine
    )
    blocks = (0 if last else others) + (groups if last and mine else others) + 2 * others
    messages = groups * CORES - 1 + segs // CORES - 1
    return (
        lanes * vectors // 256 + blocks * block
        + (messages * 4 * vectors + 2 * (groups * segs - 1) * vectors) * vectors // 256
    )


def kernel(
    groups, segs, total,
    tiles_hbm, row_hbm, col_hbm, count_hbm, energies_hbm, basis_hbm, prev_hbm, beta_prev_hbm,
    stack_ref, alpha_ref, known_ref, wide_ref, sums_ref,
    tiles, highs, lows, rows, cols, count, energies, own, far, prev, beta_prev,
    own_split, far_split, products, back, relay, forth, arrived, rest, near, late, mids, lasts,
    bulk, in_sem, tile_sem, sent, came, ready,
):
    g, p = lax.axis_index("grp"), lax.axis_index("pos")
    slots, width = tiles.shape[0], tiles.shape[-1]
    vectors, length = own.shape
    sides = length // width
    part = length // groups
    chips, devices = segs // CORES, groups * segs
    core, chip = lax.rem(p, CORES), p // CORES
    step = slots // tile_sem.shape[0]
    others = groups - 1
    FAR, CROSS, BACK, FORTH, GATHER, NEAR, LATE, MIDS, LASTS = range(9)

    def at(group, pos):
        return (group, lax.rem(pos + segs, segs))

    def partner(d):
        return flipped(g, d, groups)

    def send(src, dst, send_sem, recv_sem, to):
        return pltpu.make_async_remote_copy(
            src_ref=src, dst_ref=dst, send_sem=send_sem, recv_sem=recv_sem,
            device_id=to, device_id_type=MESH,
        )

    def post(which, src, dst, to):
        return send(src, dst, sent, came.at[which], to)

    def landed(which, ref):
        pltpu.make_async_copy(ref, ref, came.at[which]).wait()

    def all_gone(mine, last):
        ref = bulk.at[pl.ds(0, sent_kib(groups, segs, vectors, length, mine, last))]
        pltpu.make_async_copy(ref, ref, sent).wait()

    def settle_back():
        whole = jnp.logical_and(p >= segs - CORES, g != 0)
        pl.when(whole)(lambda: landed(BACK, arrived.at[pl.ds(0, groups)]))
        pl.when(jnp.logical_not(whole))(lambda: landed(BACK, arrived.at[pl.ds(0, others)]))

    mates = [(d, c) for d in reversed(range(groups)) for c in range(CORES) if d or c]

    def mate(d, c):
        return (partner(d), flipped(p, c, CORES))

    barrier = pltpu.get_barrier_semaphore()

    def greet(to):
        pl.semaphore_signal(barrier, inc=1, device_id=to, device_id_type=MESH)

    greeted = [0] * groups
    for mine in range(1, groups):
        for source, _, _ in sources(mine, length):
            greeted[source] += 1

        @pl.when(g == mine)
        def _():
            for source, _, _ in sources(mine, length):
                greet(at(source, p + mine))

    last_chip = p >= segs - CORES

    def of_last_chip(pos):
        return lax.rem(pos + segs, segs) >= segs - CORES

    for d in range(1, groups):
        @pl.when(jnp.logical_and(g != d, of_last_chip(p - d)))
        def _():
            greet(at(d, p - d))

    column = sorted({CORES * d for d in range(1, chips)} | {segs - d for d in range(1, groups)})
    for d in column:
        greet(at(g, p + d))
    for d, c in mates:
        greet(mate(d, c))

    small = [
        pltpu.make_async_copy(src, dst, in_sem.at[i])
        for i, (src, dst) in enumerate([
            (basis_hbm, own), (row_hbm, rows), (col_hbm, cols), (count_hbm, count),
            (prev_hbm, prev), (energies_hbm, energies), (beta_prev_hbm, beta_prev),
        ])
    ]
    for copy in small:
        copy.start()

    def tile_copy(i):
        some = pl.ds(i * step, step)
        return pltpu.make_async_copy(tiles_hbm.at[some], tiles.at[some], tile_sem.at[i])

    for i in range(slots // step):
        tile_copy(i).start()

    def stack(ref, out):
        for t in range(sides):
            high, low = split(ref[:, t * width : (t + 1) * width])
            out[t] = jnp.concatenate([high, low], axis=0)

    def multiply(picked, high, low, dims):
        both_parts = lax.dot_general(picked, high, dims, preferred_element_type=f32)
        both_parts += lax.dot_general(picked, low, dims, preferred_element_type=f32)
        return both_parts[:vectors] + both_parts[vectors:]

    def added(index, t):
        value = jnp.zeros((vectors, width), f32)
        for k in range(slots):
            live = jnp.logical_and(index[0, k] == t, k < count[0, 0])
            value = value + products[k] * jnp.where(live, 1.0, 0.0).astype(f32)
        return value

    def scatter(index, out, then=lambda d: None):
        whole = part // width
        for d in reversed(range(groups)):
            for t in range(whole):
                h = partner(d)
                out[h, :, t * width : (t + 1) * width] = added(index, h * whole + t)
            if whole:
                then(d)
        if not whole:
            for t in range(sides):
                value = added(index, t)
                for c in range(0, width, part):
                    out[(t * width + c) // part] = value[:, c : c + part]
            for d in reversed(range(groups)):
                then(d)

    def far_copy(to_group, i):
        _, first, lanes = sources(to_group, length)[i]
        lanes = slice(first, first + lanes)
        return post(FAR, own.at[:, lanes], far.at[:, lanes], at(to_group, p - to_group + segs))

    far_copies = [
        (source, to_group, i)
        for to_group in reversed(range(1, groups))
        for i, (source, _, _) in enumerate(sources(to_group, length))
    ]

    def backward():
        with jax.named_scope("ph_small"):
            for copy in small[1:4]:
                copy.wait()
        stack(own, own_split)

        def some(i, carry):
            tile_copy(i).wait()
            for j in range(step):
                k = i * step + j
                high, low = split(tiles[k])
                products[k] = multiply(own_split[rows[0, k]], high, low, NN)
            return carry

        with jax.named_scope("ph_bwd"):
            lax.fori_loop(0, slots // step, some, 0)
        scatter(cols, back)

    early = p < segs // 2
    small[0].wait()
    pl.when(early)(backward)
    with jax.named_scope("ph_barrier"):
        for mine in range(groups):
            expected = greeted[mine] + len(column) + len(mates)
            for last in (True, False):
                @pl.when(jnp.logical_and(g == mine, last_chip == last))
                def _():
                    pl.semaphore_wait(barrier, expected + (others if last and mine else 0))

    for last in (True, False):
        for source, to_group, i in far_copies:
            turn = of_last_chip(p - to_group) == last
            pl.when(jnp.logical_and(g == source, turn))(far_copy(to_group, i).start)
    for d in range(1, chips):
        pl.semaphore_signal(ready, inc=1, device_id=at(g, p + CORES * d), device_id_type=MESH)
    pl.when(jnp.logical_not(early))(backward)

    @pl.when(jnp.logical_not(last_chip))
    def _():
        for d in reversed(range(1, groups)):
            post(CROSS, back.at[partner(d)], relay.at[d], at(partner(d), p)).start()

    @pl.when(g == 0)
    def _():
        far[...] = own[...]

    with jax.named_scope("ph_pre"):
        for copy in small[4:]:
            copy.wait()
        lanes = pl.ds(pl.multiple_of(g * part, part), part)
        basis_part, prev_part = own[:, lanes], prev[:, lanes]
        weighted = energies[:, lanes] * basis_part
        both = jnp.concatenate([basis_part, weighted, prev_part], axis=0)
        inner = exact(both, basis_part, NT)
        inner = jnp.concatenate(
            [
                inner[: 2 * vectors],
                exact(beta_prev[...], inner[2 * vectors :], NN),
                jnp.zeros((vectors, vectors), f32),
            ],
            axis=0,
        )
        offset = weighted - exact(beta_prev[...], prev_part, NN)
        slot = g * CORES + core
        near[slot] = packed(inner)
    for d, c in mates:
        post(NEAR, near.at[slot], near.at[slot], mate(d, c)).start()

    @pl.when(last_chip)
    def _():
        for d in reversed(range(groups)):
            @pl.when(jnp.logical_or(g != 0, d != 0))
            def _():
                post(BACK, back.at[partner(d)], arrived.at[d], at(partner(d), p + g)).start()

        @pl.when(g == 0)
        def _():
            arrived[0] = back[0]

    pairs = 2 if slots % 2 == 0 else 1

    def turn(i, carry):
        for j in range(pairs):
            k = i * pairs + j
            highs[k], lows[k] = split(tiles[k].T)
        return carry

    with jax.named_scope("ph_turn"):
        lax.fori_loop(0, slots // pairs, turn, 0)

    def relay_on():
        with jax.named_scope("ph_cross"):
            landed(CROSS, relay.at[pl.ds(1, others)])
        for d in reversed(range(1, groups)):
            pl.when(g != d)(post(BACK, relay.at[d], arrived.at[d], at(g, p + partner(d))).start)
        pl.when(g != 0)(post(BACK, back.at[g], arrived.at[0], at(g, p + g)).start)
        for d in range(groups):
            @pl.when(g == d)
            def _():
                arrived[d] = relay[d] if d else back[0]

    pl.when(early)(relay_on)

    with jax.named_scope("ph_farwait"):
        pl.when(g != 0)(lambda: landed(FAR, far))

    stack(far, far_split)

    with jax.named_scope("ph_fwd"):
        for k in range(slots):
            products[k] = multiply(far_split[cols[0, k]], highs[k], lows[k], NN)
    with jax.named_scope("ph_scat2"):
        def pass_on(d):
            if d:
                post(FORTH, forth.at[partner(d)], arrived.at[groups + d - 1], at(partner(d), p)).start()

        scatter(rows, forth, pass_on)
    pl.when(jnp.logical_not(jnp.logical_or(early, last_chip)))(relay_on)

    def to_all(which, buffer, value):
        me = g * segs + p
        buffer[me] = value

        def copy(dg, dp):
            return post(which, buffer.at[me], buffer.at[me], (flipped(g, dg, groups), flipped(p, dp, segs)))

        if devices <= 64:
            apart = [
                (dp * CORES + c, dg)
                for dp in reversed(range(chips)) for dg in reversed(range(groups)) for c in range(CORES)
            ]
            apart.remove((0, 0))
            for dp, dg in apart:
                copy(dg, dp).start()
        else:
            def one(d, carry):
                copy(d // segs, lax.rem(d, segs)).start()
                return carry

            lax.fori_loop(1, devices, one, 0)

    def summed(buffer):
        value = buffer[0]
        for i in range(1, buffer.shape[0]):
            value = value + buffer[i]
        return value

    with jax.named_scope("ph_mid"):
        mid = jnp.zeros((vectors, vectors), f32)
        for h in range(groups):
            mid = mid + exact(back[h], far[:, h * part : (h + 1) * part], NT)
        pl.semaphore_wait(ready, chips - 1)
        to_all(MIDS, mids, folded(mid + mid.T))

    with jax.named_scope("ph_near"):
        landed(NEAR, near.at[pl.ds(0, groups * CORES - 1)])
        late[chip] = summed(near)
    for d in reversed(range(1, chips)):
        post(LATE, late.at[chip], late.at[chip], at(g, p + CORES * d)).start()

    with jax.named_scope("ph_kown"):
        pieces = split3(own[...])
        for i, (_, piece) in enumerate(TERMS):
            stack_ref[(2 * i + 1) * vectors : (2 * i + 2) * vectors, :] = pieces[piece]
    with jax.named_scope("ph_rswait"):
        settle_back()
        landed(FORTH, arrived.at[pl.ds(groups, others)])

    with jax.named_scope("ph_gram"):
        mine = forth[g] + offset
        for d in range(2 * groups - 1):
            mine = mine + arrived[d]
        rest[:, lanes] = mine
        value = folded(exact(mine, mine, NT))
        for d in reversed(range(1, groups)):
            post(GATHER, rest.at[:, lanes], rest.at[:, lanes], at(partner(d), p)).start()
        to_all(LASTS, lasts, value)

    with jax.named_scope("ph_latewait"):
        landed(LATE, late.at[pl.ds(0, chips - 1)])
    with jax.named_scope("ph_gatherwait"):
        landed(GATHER, rest.at[:, pl.ds(0, others * part)])
    with jax.named_scope("ph_krest"):
        pieces = split3(rest[...])
        for i, (_, piece) in enumerate(TERMS):
            stack_ref[2 * i * vectors : (2 * i + 1) * vectors, :] = pieces[piece]
    with jax.named_scope("ph_sendwait"):
        for mine in range(groups):
            for last in (True, False):
                @pl.when(jnp.logical_and(g == mine, last_chip == last))
                def _():
                    all_gone(mine, last)
    with jax.named_scope("ph_midswait"):
        landed(MIDS, mids.at[pl.ds(0, devices - 1)])
    with jax.named_scope("ph_known"):
        inner = unpacked(summed(late))
        own_own, shift = inner[:vectors], inner[2 * vectors : 3 * vectors]
        applied_own = inner[vectors : 2 * vectors] + unfolded(summed(mids), vectors)
        rest_own, alpha_t = applied_own - shift, applied_own / total
        alpha_ref[...] = alpha_t
        row_at = lax.broadcasted_iota(jnp.int32, (vectors, vectors), 0)
        col_at = lax.broadcasted_iota(jnp.int32, (vectors, vectors), 1)
        identity = jnp.where(row_at == col_at, 1.0, 0.0).astype(f32)
        wide_ref[...] = jnp.concatenate([identity, -alpha_t] * len(TERMS), axis=1)
        known_ref[...] = (
            exact(exact(alpha_t, own_own, NN) - rest_own, alpha_t, NT) - exact(alpha_t, rest_own, NT)
        )
    with jax.named_scope("ph_lastswait"):
        landed(LASTS, lasts.at[pl.ds(0, devices - 1)])
    sums_ref[...] = summed(lasts)


def finish(
    total, sums_ref, alpha_t_ref, known_ref, wide_ref, stack_ref, next_hbm, alpha_hbm, beta_hbm,
    ahead, alpha, beta, sem,
):
    vectors, length = ahead.shape
    alpha[...] = alpha_t_ref[...].T
    outs = [pltpu.make_async_copy(alpha, alpha_hbm, sem.at[0]), pltpu.make_async_copy(beta, beta_hbm, sem.at[1])]
    outs[0].start()
    gram = (unfolded(sums_ref[...], vectors) + known_ref[...]) / total
    cuts = [slice(i, min(i + LANES, wide_ref.shape[1])) for i in range(0, wide_ref.shape[1], LANES)]
    with jax.named_scope("ph_factor"):
        upper, weights = factored(gram, [wide_ref[:, cut] for cut in cuts])
    left = []
    for cut, values in zip(cuts, weights, strict=True):
        pieces = split3(values)
        term = lax.broadcasted_iota(jnp.int32, values.shape, 1) // (2 * vectors) + cut.start // (2 * vectors)
        value = pieces[0].astype(f32)
        for i, (piece, _) in enumerate(TERMS):
            if piece:
                value = jnp.where(term == i, pieces[piece].astype(f32), value)
        left.append(value.astype(bf16))
    left = jnp.concatenate(left, axis=1)
    with jax.named_scope("ph_last"):
        half = length // 2
        for i in range(2):
            lanes = slice(i * half, (i + 1) * half)
            ahead[:, lanes] = lax.dot_general(left, stack_ref[:, lanes], NN, preferred_element_type=f32)
            outs.append(pltpu.make_async_copy(ahead.at[:, lanes], next_hbm.at[:, lanes], sem.at[2 + i]))
            outs[-1].start()
    beta[...] = upper.T
    outs[1].start()
    for copy in outs:
        copy.wait()


def shards(groups, segs, tiles, tile_row, tile_col, tile_count, energies, basis, prev_basis, beta_prev):
    slots, width = tiles.shape[2], tiles.shape[-1]
    vectors, length = basis.shape
    sides, part, chips = length // width, length // groups, segs // CORES
    step = next(n for n in (4, 3, 2, 1) if slots % n == 0)
    total = float(length * segs)
    dma = pltpu.SemaphoreType.DMA
    block, square = (vectors, length), (vectors, vectors)
    message, fold = (vectors // 2, 8 * vectors), (vectors * vectors // LANES, LANES)
    kib = max(
        sent_kib(groups, segs, vectors, length, mine, last)
        for mine in range(groups) for last in (True, False)
    )
    vmem = pl.BlockSpec(memory_space=pltpu.VMEM)
    stack, alpha_t, known, wide, sums = pl.pallas_call(
        functools.partial(kernel, groups, segs, total),
        out_shape=(
            pltpu.VMEM((2 * len(TERMS) * vectors, length), bf16),
            pltpu.VMEM(square, f32),
            pltpu.VMEM(square, f32),
            pltpu.VMEM((vectors, 2 * len(TERMS) * vectors), f32),
            pltpu.VMEM(fold, f32),
        ),
        in_specs=[pl.BlockSpec(memory_space=pltpu.HBM)] * 8,
        out_specs=(vmem,) * 5,
        scratch_shapes=[
            pltpu.VMEM((slots, width, width), f32),
            pltpu.VMEM((slots, width, width), bf16),
            pltpu.VMEM((slots, width, width), bf16),
            pltpu.SMEM((1, slots), jnp.int32),
            pltpu.SMEM((1, slots), jnp.int32),
            pltpu.SMEM((1, 1), jnp.int32),
            pltpu.VMEM((1, length), f32),
            pltpu.VMEM(block, f32),
            pltpu.VMEM(block, f32),
            pltpu.VMEM(block, f32),
            pltpu.VMEM(square, f32),
            pltpu.VMEM((sides, 2 * vectors, width), bf16),
            pltpu.VMEM((sides, 2 * vectors, width), bf16),
            pltpu.VMEM((slots, vectors, width), f32),
            pltpu.VMEM((groups, vectors, part), f32),
            pltpu.VMEM((groups, vectors, part), f32),
            pltpu.VMEM((groups, vectors, part), f32),
            pltpu.VMEM((2 * groups - 1, vectors, part), f32),
            pltpu.VMEM(block, f32),
            pltpu.VMEM((groups * CORES, *message), f32),
            pltpu.VMEM((chips, *message), f32),
            pltpu.VMEM((groups * segs, *fold), f32),
            pltpu.VMEM((groups * segs, *fold), f32),
            pltpu.VMEM((kib, *fold), f32),
            dma((7,)), dma((slots // step,)), dma, dma((9,)),
            pltpu.SemaphoreType.REGULAR,
        ],
        compiler_params=pltpu.CompilerParams(collective_id=0, has_side_effects=True),
    )(
        tiles.reshape(slots, width, width),
        tile_row.reshape(1, slots),
        tile_col.reshape(1, slots),
        tile_count.reshape(1, 1),
        energies.reshape(1, length),
        basis,
        prev_basis,
        beta_prev,
    )
    held = [pltpu.with_memory_space_constraint(x, pltpu.VMEM) for x in (sums, alpha_t, known, wide, stack)]
    return pl.pallas_call(
        functools.partial(finish, total),
        out_shape=(
            jax.ShapeDtypeStruct(block, f32),
            jax.ShapeDtypeStruct(square, f32),
            jax.ShapeDtypeStruct(square, f32),
        ),
        in_specs=[vmem] * 5,
        out_specs=(pl.BlockSpec(memory_space=pltpu.HBM),) * 3,
        scratch_shapes=[pltpu.VMEM(block, f32), pltpu.VMEM(square, f32), pltpu.VMEM(square, f32), dma((4,))],
    )(*held)


def solution(mesh):
    groups, segs = mesh.shape["grp"], mesh.shape["pos"]
    in_specs = (
        P("grp", "pos", None, None, None),
        P("grp", "pos", None),
        P("grp", "pos", None),
        P("grp", "pos"),
        P("pos"),
        P(None, "pos"),
        P(None, "pos"),
        P(),
    )
    out_specs = (P(None, "pos"), P(), P())
    return jax.shard_map(
        functools.partial(shards, groups, segs),
        mesh=mesh, in_specs=in_specs, out_specs=out_specs, check_vma=False,
    )
```

```python
import functools

import jax
import jax.numpy as jnp
from jax import lax
from jax.experimental import pallas as pl
from jax.experimental.pallas import tpu as pltpu
from jax.sharding import PartitionSpec as P

MESH = pl.DeviceIdType.MESH
NT = (((1,), (1,)), ((), ()))
NN = (((1,), (0,)), ((), ()))
f32 = jnp.float32
bf16 = jnp.bfloat16
CORES = 2
LANES = 128
TERMS = ((0, 0), (0, 1), (1, 0), (0, 2), (2, 0), (1, 1))


def exact(left, right, dims):
    return lax.dot_general(
        left, right, dims, precision=lax.Precision.HIGHEST, preferred_element_type=f32
    )


def split(values):
    high = values.astype(bf16)
    return high, (values - high.astype(f32)).astype(bf16)


def split3(values):
    high = values.astype(bf16)
    rest = values - high.astype(f32)
    middle = rest.astype(bf16)
    return high, middle, (rest - middle.astype(f32)).astype(bf16)


def packed(values):
    rows = values.shape[0] // 8
    return jnp.concatenate([values[i * rows : (i + 1) * rows] for i in range(8)], axis=1)


def unpacked(values):
    lanes = values.shape[1] // 8
    return jnp.concatenate([values[:, i * lanes : (i + 1) * lanes] for i in range(8)], axis=0)


def folded(values):
    rows = values.size // LANES
    return jnp.concatenate([values[i : i + rows] for i in range(0, values.shape[0], rows)], axis=1)


def unfolded(values, lanes):
    return jnp.concatenate([values[:, i : i + lanes] for i in range(0, LANES, lanes)], axis=0)


def sources(group, length):
    half, quarter = length // 2, length // 4
    low, high = group & (group - 1), group - (1 << (group.bit_length() - 1))
    if low == high:
        own = half + quarter if group == 1 else half
        return [(group, 0, own), (low, own, length - own)]
    return [(group, 0, half), (low, half, quarter), (high, half + quarter, quarter)]


def factored(gram, wide):
    n = gram.shape[0]
    wide = [*wide, gram]
    row_at = lax.broadcasted_iota(jnp.int32, (n, 1), 0)
    columns = [jnp.broadcast_to(gram[:, k : k + 1], (n, LANES)) for k in range(n)]
    done = [jnp.zeros(x.shape, f32) for x in wide]
    for j in range(n):
        corner = columns[j][j : j + 1]
        inverse, root = 1.0 / corner, lax.rsqrt(corner)
        for i, x in enumerate(wide):
            lanes = x.shape[1]
            row = x[j : j + 1]
            done[i] = jnp.where(row_at == j, row * root[:, :lanes], done[i])
            wide[i] = x - columns[j][:, :lanes] * (row * inverse[:, :lanes])
        for k in range(j + 1, n):
            columns[k] = columns[k] - columns[j] * (columns[k][j : j + 1] * inverse)
    return done[-1], done[:-1]


def flipped(value, d, count):
    out, bit = value, 1
    while bit < count:
        if not isinstance(d, int) or d & bit:
            out = out + (d // bit % 2) * (bit - 2 * bit * lax.rem(value // bit, 2))
        bit *= 2
    return out


def sent_kib(groups, segs, vectors, length, mine, last):
    others, block = groups - 1, vectors * length // groups // 256
    lanes = sum(
        n for to_group in range(1, groups)
        for source, _, n in sources(to_group, length) if source == mine
    )
    blocks = (0 if last else others) + (groups if last and mine else others) + 2 * others
    messages = groups * CORES - 1 + segs // CORES - 1
    return (
        lanes * vectors // 256 + blocks * block
        + (messages * 5 * vectors + (groups * segs - 1) * vectors) * vectors // 256
    )


def kernel(
    groups, segs, total,
    tiles_hbm, row_hbm, col_hbm, count_hbm, energies_hbm, basis_hbm, prev_hbm, beta_prev_hbm,
    stack_ref, alpha_ref, known_ref, wide_ref, sums_ref,
    tiles, highs, lows, rows, cols, count, energies, own, far, prev, beta_prev,
    own_split, far_split, products, back, relay, forth, arrived, rest, near, late, mids, ends, lasts,
    bulk, in_sem, tile_sem, sent, came, ready,
):
    g, p = lax.axis_index("grp"), lax.axis_index("pos")
    slots, width = tiles.shape[0], tiles.shape[-1]
    vectors, length = own.shape
    sides = length // width
    part = length // groups
    chips, devices = segs // CORES, groups * segs
    core, chip = lax.rem(p, CORES), p // CORES
    step = slots // tile_sem.shape[0]
    others = groups - 1
    FAR, CROSS, BACK, FORTH, GATHER, NEAR, LATE, MIDS, ENDS, LASTS = range(10)

    def at(group, pos):
        return (group, lax.rem(pos + segs, segs))

    def partner(d):
        return flipped(g, d, groups)

    def send(src, dst, send_sem, recv_sem, to):
        return pltpu.make_async_remote_copy(
            src_ref=src, dst_ref=dst, send_sem=send_sem, recv_sem=recv_sem,
            device_id=to, device_id_type=MESH,
        )

    def post(which, src, dst, to):
        return send(src, dst, sent, came.at[which], to)

    def landed(which, ref):
        pltpu.make_async_copy(ref, ref, came.at[which]).wait()

    def all_gone(mine, last):
        ref = bulk.at[pl.ds(0, sent_kib(groups, segs, vectors, length, mine, last))]
        pltpu.make_async_copy(ref, ref, sent).wait()

    def settle_back():
        whole = jnp.logical_and(p >= segs - CORES, g != 0)
        pl.when(whole)(lambda: landed(BACK, arrived.at[pl.ds(0, groups)]))
        pl.when(jnp.logical_not(whole))(lambda: landed(BACK, arrived.at[pl.ds(0, others)]))

    mates = [(d, c) for d in reversed(range(groups)) for c in range(CORES) if d or c]

    def mate(d, c):
        return (partner(d), flipped(p, c, CORES))

    barrier = pltpu.get_barrier_semaphore()

    def greet(to):
        pl.semaphore_signal(barrier, inc=1, device_id=to, device_id_type=MESH)

    greeted = [0] * groups
    for mine in range(1, groups):
        for source, _, _ in sources(mine, length):
            greeted[source] += 1

        @pl.when(g == mine)
        def _():
            for source, _, _ in sources(mine, length):
                greet(at(source, p + mine))

    last_chip = p >= segs - CORES

    def of_last_chip(pos):
        return lax.rem(pos + segs, segs) >= segs - CORES

    for d in range(1, groups):
        @pl.when(jnp.logical_and(g != d, of_last_chip(p - d)))
        def _():
            greet(at(d, p - d))

    column = sorted({CORES * d for d in range(1, chips)} | {segs - d for d in range(1, groups)})
    for d in column:
        greet(at(g, p + d))
    for d, c in mates:
        greet(mate(d, c))

    small = [
        pltpu.make_async_copy(src, dst, in_sem.at[i])
        for i, (src, dst) in enumerate([
            (basis_hbm, own), (row_hbm, rows), (col_hbm, cols), (count_hbm, count),
            (prev_hbm, prev), (energies_hbm, energies), (beta_prev_hbm, beta_prev),
        ])
    ]
    for copy in small:
        copy.start()

    def tile_copy(i):
        some = pl.ds(i * step, step)
        return pltpu.make_async_copy(tiles_hbm.at[some], tiles.at[some], tile_sem.at[i])

    for i in range(slots // step):
        tile_copy(i).start()

    def stack(ref, out):
        for t in range(sides):
            high, low = split(ref[:, t * width : (t + 1) * width])
            out[t] = jnp.concatenate([high, low], axis=0)

    def multiply(picked, high, low, dims):
        both_parts = lax.dot_general(picked, high, dims, preferred_element_type=f32)
        both_parts += lax.dot_general(picked, low, dims, preferred_element_type=f32)
        return both_parts[:vectors] + both_parts[vectors:]

    def added(index, t):
        value = jnp.zeros((vectors, width), f32)
        for k in range(slots):
            live = jnp.logical_and(index[0, k] == t, k < count[0, 0])
            value = value + products[k] * jnp.where(live, 1.0, 0.0).astype(f32)
        return value

    def scatter(index, out, then=lambda d: None):
        whole = part // width
        for d in reversed(range(groups)):
            for t in range(whole):
                h = partner(d)
                out[h, :, t * width : (t + 1) * width] = added(index, h * whole + t)
            if whole:
                then(d)
        if not whole:
            for t in range(sides):
                value = added(index, t)
                for c in range(0, width, part):
                    out[(t * width + c) // part] = value[:, c : c + part]
            for d in reversed(range(groups)):
                then(d)

    def far_copy(to_group, i):
        _, first, lanes = sources(to_group, length)[i]
        lanes = slice(first, first + lanes)
        return post(FAR, own.at[:, lanes], far.at[:, lanes], at(to_group, p - to_group + segs))

    far_copies = [
        (source, to_group, i)
        for to_group in reversed(range(1, groups))
        for i, (source, _, _) in enumerate(sources(to_group, length))
    ]

    def backward():
        with jax.named_scope("ph_small"):
            for copy in small[1:4]:
                copy.wait()
        stack(own, own_split)

        def some(i, carry):
            tile_copy(i).wait()
            for j in range(step):
                k = i * step + j
                high, low = split(tiles[k])
                products[k] = multiply(own_split[rows[0, k]], high, low, NN)
            return carry

        with jax.named_scope("ph_bwd"):
            lax.fori_loop(0, slots // step, some, 0)
        scatter(cols, back)

    early = p < segs // 2
    small[0].wait()
    pl.when(early)(backward)
    with jax.named_scope("ph_barrier"):
        for mine in range(groups):
            expected = greeted[mine] + len(column) + len(mates)
            for last in (True, False):
                @pl.when(jnp.logical_and(g == mine, last_chip == last))
                def _():
                    pl.semaphore_wait(barrier, expected + (others if last and mine else 0))

    for last in (True, False):
        for source, to_group, i in far_copies:
            turn = of_last_chip(p - to_group) == last
            pl.when(jnp.logical_and(g == source, turn))(far_copy(to_group, i).start)
    for d in range(1, chips):
        pl.semaphore_signal(ready, inc=1, device_id=at(g, p + CORES * d), device_id_type=MESH)
    pl.when(jnp.logical_not(early))(backward)

    @pl.when(jnp.logical_not(last_chip))
    def _():
        for d in reversed(range(1, groups)):
            post(CROSS, back.at[partner(d)], relay.at[d], at(partner(d), p)).start()

    @pl.when(g == 0)
    def _():
        far[...] = own[...]

    with jax.named_scope("ph_pre"):
        for copy in small[4:]:
            copy.wait()
        lanes = pl.ds(pl.multiple_of(g * part, part), part)
        basis_part, prev_part = own[:, lanes], prev[:, lanes]
        weighted = energies[:, lanes] * basis_part
        both = jnp.concatenate([basis_part, weighted, prev_part], axis=0)
        inner = exact(both, basis_part, NT)
        inner = jnp.concatenate(
            [
                inner[: 2 * vectors],
                exact(beta_prev[...], inner[2 * vectors :], NN),
                jnp.zeros((vectors, vectors), f32),
            ],
            axis=0,
        )
        offset = weighted - exact(beta_prev[...], prev_part, NN)
        slot = g * CORES + core
        near[slot] = packed(inner)
    for d, c in mates:
        post(NEAR, near.at[slot], near.at[slot], mate(d, c)).start()

    @pl.when(last_chip)
    def _():
        for d in reversed(range(groups)):
            @pl.when(jnp.logical_or(g != 0, d != 0))
            def _():
                post(BACK, back.at[partner(d)], arrived.at[d], at(partner(d), p + g)).start()

        @pl.when(g == 0)
        def _():
            arrived[0] = back[0]

    pairs = 2 if slots % 2 == 0 else 1

    def turn(i, carry):
        for j in range(pairs):
            k = i * pairs + j
            highs[k], lows[k] = split(tiles[k].T)
        return carry

    with jax.named_scope("ph_turn"):
        lax.fori_loop(0, slots // pairs, turn, 0)

    def relay_on():
        with jax.named_scope("ph_cross"):
            landed(CROSS, relay.at[pl.ds(1, others)])
        for d in reversed(range(1, groups)):
            pl.when(g != d)(post(BACK, relay.at[d], arrived.at[d], at(g, p + partner(d))).start)
        pl.when(g != 0)(post(BACK, back.at[g], arrived.at[0], at(g, p + g)).start)
        for d in range(groups):
            @pl.when(g == d)
            def _():
                arrived[d] = relay[d] if d else back[0]

    pl.when(early)(relay_on)

    with jax.named_scope("ph_farwait"):
        pl.when(g != 0)(lambda: landed(FAR, far))

    stack(far, far_split)

    with jax.named_scope("ph_fwd"):
        for k in range(slots):
            products[k] = multiply(far_split[cols[0, k]], highs[k], lows[k], NN)
    with jax.named_scope("ph_scat2"):
        def pass_on(d):
            if d:
                post(FORTH, forth.at[partner(d)], arrived.at[groups + d - 1], at(partner(d), p)).start()

        scatter(rows, forth, pass_on)
    pl.when(jnp.logical_not(jnp.logical_or(early, last_chip)))(relay_on)

    def to_all(which, buffer, value):
        me = g * segs + p
        buffer[me] = value

        def copy(dg, dp):
            return post(which, buffer.at[me], buffer.at[me], (flipped(g, dg, groups), flipped(p, dp, segs)))

        if devices <= 64:
            apart = [
                (dp * CORES + c, dg)
                for dp in reversed(range(chips)) for dg in reversed(range(groups)) for c in range(CORES)
            ]
            apart.remove((0, 0))
            for dp, dg in apart:
                copy(dg, dp).start()
        else:
            def one(d, carry):
                copy(d // segs, lax.rem(d, segs)).start()
                return carry

            lax.fori_loop(1, devices, one, 0)

    def summed(buffer):
        value = buffer[0]
        for i in range(1, buffer.shape[0]):
            value = value + buffer[i]
        return value

    with jax.named_scope("ph_mid"):
        mid = jnp.zeros((vectors, vectors), f32)
        for h in range(groups):
            mid = mid + exact(back[h], far[:, h * part : (h + 1) * part], NT)
        mids[chip] = folded(mid + mid.T)
    for d in reversed(range(1, chips)):
        post(MIDS, mids.at[chip], mids.at[chip], at(g, p + CORES * d)).start()

    with jax.named_scope("ph_near"):
        landed(NEAR, near.at[pl.ds(0, groups * CORES - 1)])
        late[chip] = summed(near)
    for d in reversed(range(1, chips)):
        post(LATE, late.at[chip], late.at[chip], at(g, p + CORES * d)).start()

    with jax.named_scope("ph_kown"):
        pieces = split3(own[...])
        for i, (_, piece) in enumerate(TERMS):
            stack_ref[(2 * i + 1) * vectors : (2 * i + 2) * vectors, :] = pieces[piece]
    with jax.named_scope("ph_rswait"):
        settle_back()
        landed(FORTH, arrived.at[pl.ds(groups, others)])

    with jax.named_scope("ph_gram"):
        pl.semaphore_wait(ready, chips - 1)
        mine = forth[g] + offset
        for d in range(2 * groups - 1):
            mine = mine + arrived[d]
        rest[:, lanes] = mine
        value = folded(exact(mine, mine, NT))
        for d in reversed(range(1, groups)):
            post(GATHER, rest.at[:, lanes], rest.at[:, lanes], at(partner(d), p)).start()
        to_all(LASTS, lasts, value)

    with jax.named_scope("ph_latewait"):
        landed(LATE, late.at[pl.ds(0, chips - 1)])
    with jax.named_scope("ph_mids1"):
        landed(MIDS, mids.at[pl.ds(0, chips - 1)])
        ends[slot] = summed(mids)
    for d, c in mates:
        post(ENDS, ends.at[slot], ends.at[slot], mate(d, c)).start()
    with jax.named_scope("ph_gatherwait"):
        landed(GATHER, rest.at[:, pl.ds(0, others * part)])
    with jax.named_scope("ph_krest"):
        pieces = split3(rest[...])
        for i, (_, piece) in enumerate(TERMS):
            stack_ref[2 * i * vectors : (2 * i + 1) * vectors, :] = pieces[piece]
    with jax.named_scope("ph_sendwait"):
        for mine in range(groups):
            for last in (True, False):
                @pl.when(jnp.logical_and(g == mine, last_chip == last))
                def _():
                    all_gone(mine, last)
    with jax.named_scope("ph_midswait"):
        landed(ENDS, ends.at[pl.ds(0, groups * CORES - 1)])
    with jax.named_scope("ph_known"):
        inner = unpacked(summed(late))
        own_own, shift = inner[:vectors], inner[2 * vectors : 3 * vectors]
        applied_own = inner[vectors : 2 * vectors] + unfolded(summed(ends), vectors)
        rest_own, alpha_t = applied_own - shift, applied_own / total
        alpha_ref[...] = alpha_t
        row_at = lax.broadcasted_iota(jnp.int32, (vectors, vectors), 0)
        col_at = lax.broadcasted_iota(jnp.int32, (vectors, vectors), 1)
        identity = jnp.where(row_at == col_at, 1.0, 0.0).astype(f32)
        wide_ref[...] = jnp.concatenate([identity, -alpha_t] * len(TERMS), axis=1)
        known_ref[...] = (
            exact(exact(alpha_t, own_own, NN) - rest_own, alpha_t, NT) - exact(alpha_t, rest_own, NT)
        )
    with jax.named_scope("ph_lastswait"):
        landed(LASTS, lasts.at[pl.ds(0, devices - 1)])
    sums_ref[...] = summed(lasts)


def finish(
    total, sums_ref, alpha_t_ref, known_ref, wide_ref, stack_ref, next_hbm, alpha_hbm, beta_hbm,
    ahead, alpha, beta, sem,
):
    vectors, length = ahead.shape
    alpha[...] = alpha_t_ref[...].T
    outs = [pltpu.make_async_copy(alpha, alpha_hbm, sem.at[0]), pltpu.make_async_copy(beta, beta_hbm, sem.at[1])]
    outs[0].start()
    gram = (unfolded(sums_ref[...], vectors) + known_ref[...]) / total
    cuts = [slice(i, min(i + LANES, wide_ref.shape[1])) for i in range(0, wide_ref.shape[1], LANES)]
    with jax.named_scope("ph_factor"):
        upper, weights = factored(gram, [wide_ref[:, cut] for cut in cuts])
    left = []
    for cut, values in zip(cuts, weights, strict=True):
        pieces = split3(values)
        term = lax.broadcasted_iota(jnp.int32, values.shape, 1) // (2 * vectors) + cut.start // (2 * vectors)
        value = pieces[0].astype(f32)
        for i, (piece, _) in enumerate(TERMS):
            if piece:
                value = jnp.where(term == i, pieces[piece].astype(f32), value)
        left.append(value.astype(bf16))
    left = jnp.concatenate(left, axis=1)
    with jax.named_scope("ph_last"):
        half = length // 2
        for i in range(2):
            lanes = slice(i * half, (i + 1) * half)
            ahead[:, lanes] = lax.dot_general(left, stack_ref[:, lanes], NN, preferred_element_type=f32)
            outs.append(pltpu.make_async_copy(ahead.at[:, lanes], next_hbm.at[:, lanes], sem.at[2 + i]))
            outs[-1].start()
            if i == 0:
                beta[...] = upper.T
                outs[1].start()
    for copy in outs:
        copy.wait()


def shards(groups, segs, tiles, tile_row, tile_col, tile_count, energies, basis, prev_basis, beta_prev):
    slots, width = tiles.shape[2], tiles.shape[-1]
    vectors, length = basis.shape
    sides, part, chips = length // width, length // groups, segs // CORES
    step = next(n for n in (4, 3, 2, 1) if slots % n == 0)
    total = float(length * segs)
    dma = pltpu.SemaphoreType.DMA
    block, square = (vectors, length), (vectors, vectors)
    message, fold = (vectors // 2, 8 * vectors), (vectors * vectors // LANES, LANES)
    kib = max(
        sent_kib(groups, segs, vectors, length, mine, last)
        for mine in range(groups) for last in (True, False)
    )
    vmem = pl.BlockSpec(memory_space=pltpu.VMEM)
    stack, alpha_t, known, wide, sums = pl.pallas_call(
        functools.partial(kernel, groups, segs, total),
        out_shape=(
            pltpu.VMEM((2 * len(TERMS) * vectors, length), bf16),
            pltpu.VMEM(square, f32),
            pltpu.VMEM(square, f32),
            pltpu.VMEM((vectors, 2 * len(TERMS) * vectors), f32),
            pltpu.VMEM(fold, f32),
        ),
        in_specs=[pl.BlockSpec(memory_space=pltpu.HBM)] * 8,
        out_specs=(vmem,) * 5,
        scratch_shapes=[
            pltpu.VMEM((slots, width, width), f32),
            pltpu.VMEM((slots, width, width), bf16),
            pltpu.VMEM((slots, width, width), bf16),
            pltpu.SMEM((1, slots), jnp.int32),
            pltpu.SMEM((1, slots), jnp.int32),
            pltpu.SMEM((1, 1), jnp.int32),
            pltpu.VMEM((1, length), f32),
            pltpu.VMEM(block, f32),
            pltpu.VMEM(block, f32),
            pltpu.VMEM(block, f32),
            pltpu.VMEM(square, f32),
            pltpu.VMEM((sides, 2 * vectors, width), bf16),
            pltpu.VMEM((sides, 2 * vectors, width), bf16),
            pltpu.VMEM((slots, vectors, width), f32),
            pltpu.VMEM((groups, vectors, part), f32),
            pltpu.VMEM((groups, vectors, part), f32),
            pltpu.VMEM((groups, vectors, part), f32),
            pltpu.VMEM((2 * groups - 1, vectors, part), f32),
            pltpu.VMEM(block, f32),
            pltpu.VMEM((groups * CORES, *message), f32),
            pltpu.VMEM((chips, *message), f32),
            pltpu.VMEM((chips, *fold), f32),
            pltpu.VMEM((groups * CORES, *fold), f32),
            pltpu.VMEM((groups * segs, *fold), f32),
            pltpu.VMEM((kib, *fold), f32),
            dma((7,)), dma((slots // step,)), dma, dma((10,)),
            pltpu.SemaphoreType.REGULAR,
        ],
        compiler_params=pltpu.CompilerParams(collective_id=0, has_side_effects=True),
    )(
        tiles.reshape(slots, width, width),
        tile_row.reshape(1, slots),
        tile_col.reshape(1, slots),
        tile_count.reshape(1, 1),
        energies.reshape(1, length),
        basis,
        prev_basis,
        beta_prev,
    )
    held = [pltpu.with_memory_space_constraint(x, pltpu.VMEM) for x in (sums, alpha_t, known, wide, stack)]
    return pl.pallas_call(
        functools.partial(finish, total),
        out_shape=(
            jax.ShapeDtypeStruct(block, f32),
            jax.ShapeDtypeStruct(square, f32),
            jax.ShapeDtypeStruct(square, f32),
        ),
        in_specs=[vmem] * 5,
        out_specs=(pl.BlockSpec(memory_space=pltpu.HBM),) * 3,
        scratch_shapes=[pltpu.VMEM(block, f32), pltpu.VMEM(square, f32), pltpu.VMEM(square, f32), dma((4,))],
    )(*held)


def solution(mesh):
    groups, segs = mesh.shape["grp"], mesh.shape["pos"]
    in_specs = (
        P("grp", "pos", None, None, None),
        P("grp", "pos", None),
        P("grp", "pos", None),
        P("grp", "pos"),
        P("pos"),
        P(None, "pos"),
        P(None, "pos"),
        P(),
    )
    out_specs = (P(None, "pos"), P(), P())
    return jax.shard_map(
        functools.partial(shards, groups, segs),
        mesh=mesh, in_specs=in_specs, out_specs=out_specs, check_vma=False,
    )
```

```python
import functools

import jax
import jax.numpy as jnp
from jax import lax
from jax.experimental import pallas as pl
from jax.experimental.pallas import tpu as pltpu
from jax.sharding import PartitionSpec as P

MESH = pl.DeviceIdType.MESH
NT = (((1,), (1,)), ((), ()))
NN = (((1,), (0,)), ((), ()))
f32 = jnp.float32
bf16 = jnp.bfloat16
CORES = 2
LANES = 128
TERMS = ((0, 0), (0, 1), (1, 0), (0, 2), (2, 0), (1, 1))


def exact(left, right, dims):
    return lax.dot_general(
        left, right, dims, precision=lax.Precision.HIGHEST, preferred_element_type=f32
    )


def split(values):
    high = values.astype(bf16)
    return high, (values - high.astype(f32)).astype(bf16)


def split3(values):
    high = values.astype(bf16)
    rest = values - high.astype(f32)
    middle = rest.astype(bf16)
    return high, middle, (rest - middle.astype(f32)).astype(bf16)


def packed(values):
    rows = values.shape[0] // 8
    return jnp.concatenate([values[i * rows : (i + 1) * rows] for i in range(8)], axis=1)


def unpacked(values):
    lanes = values.shape[1] // 8
    return jnp.concatenate([values[:, i * lanes : (i + 1) * lanes] for i in range(8)], axis=0)


def folded(values):
    rows = values.size // LANES
    return jnp.concatenate([values[i : i + rows] for i in range(0, values.shape[0], rows)], axis=1)


def unfolded(values, lanes):
    return jnp.concatenate([values[:, i : i + lanes] for i in range(0, LANES, lanes)], axis=0)


def sources(group, length):
    half, quarter = length // 2, length // 4
    low, high = group & (group - 1), group - (1 << (group.bit_length() - 1))
    if low == high:
        own = half + quarter if group == 1 else half
        return [(group, 0, own), (low, own, length - own)]
    return [(group, 0, half), (low, half, quarter), (high, half + quarter, quarter)]


def factored(gram, wide):
    n = gram.shape[0]
    wide = [*wide, gram]
    row_at = lax.broadcasted_iota(jnp.int32, (n, 1), 0)
    columns = [jnp.broadcast_to(gram[:, k : k + 1], (n, LANES)) for k in range(n)]
    done = [jnp.zeros(x.shape, f32) for x in wide]
    for j in range(n):
        corner = columns[j][j : j + 1]
        inverse, root = 1.0 / corner, lax.rsqrt(corner)
        for i, x in enumerate(wide):
            lanes = x.shape[1]
            row = x[j : j + 1]
            done[i] = jnp.where(row_at == j, row * root[:, :lanes], done[i])
            wide[i] = x - columns[j][:, :lanes] * (row * inverse[:, :lanes])
        for k in range(j + 1, n):
            columns[k] = columns[k] - columns[j] * (columns[k][j : j + 1] * inverse)
    return done[-1], done[:-1]


def flipped(value, d, count):
    out, bit = value, 1
    while bit < count:
        if not isinstance(d, int) or d & bit:
            out = out + (d // bit % 2) * (bit - 2 * bit * lax.rem(value // bit, 2))
        bit *= 2
    return out


def sent_kib(groups, segs, vectors, length, mine, last):
    others, block = groups - 1, vectors * length // groups // 256
    lanes = sum(
        n for to_group in range(1, groups)
        for source, _, n in sources(to_group, length) if source == mine
    )
    blocks = (0 if last else others) + (groups if last and mine else others) + 2 * others
    messages = groups * CORES - 1 + segs // CORES - 1
    return (
        lanes * vectors // 256 + blocks * block
        + (messages * 5 * vectors + (groups * segs - 1) * vectors) * vectors // 256
    )


def kernel(
    groups, segs, total,
    tiles_hbm, row_hbm, col_hbm, count_hbm, energies_hbm, basis_hbm, prev_hbm, beta_prev_hbm,
    stack_ref, alpha_ref, known_ref, wide_ref, sums_ref,
    tiles, highs, lows, rows, cols, count, energies, own, far, prev, beta_prev,
    own_split, far_split, products, back, relay, forth, arrived, rest, near, late, mids, ends, lasts,
    bulk, in_sem, tile_sem, sent, came, ready,
):
    g, p = lax.axis_index("grp"), lax.axis_index("pos")
    slots, width = tiles.shape[0], tiles.shape[-1]
    vectors, length = own.shape
    sides = length // width
    part = length // groups
    chips, devices = segs // CORES, groups * segs
    core, chip = lax.rem(p, CORES), p // CORES
    step = slots // tile_sem.shape[0]
    others = groups - 1
    FAR, CROSS, BACK, FORTH, GATHER, NEAR, LATE, MIDS, ENDS, LASTS = range(10)

    def at(group, pos):
        return (group, lax.rem(pos + segs, segs))

    def partner(d):
        return flipped(g, d, groups)

    def send(src, dst, send_sem, recv_sem, to):
        return pltpu.make_async_remote_copy(
            src_ref=src, dst_ref=dst, send_sem=send_sem, recv_sem=recv_sem,
            device_id=to, device_id_type=MESH,
        )

    def post(which, src, dst, to):
        return send(src, dst, sent, came.at[which], to)

    def landed(which, ref):
        pltpu.make_async_copy(ref, ref, came.at[which]).wait()

    def all_gone(mine, last):
        ref = bulk.at[pl.ds(0, sent_kib(groups, segs, vectors, length, mine, last))]
        pltpu.make_async_copy(ref, ref, sent).wait()

    def settle_back():
        whole = jnp.logical_and(p >= segs - CORES, g != 0)
        pl.when(whole)(lambda: landed(BACK, arrived.at[pl.ds(0, groups)]))
        pl.when(jnp.logical_not(whole))(lambda: landed(BACK, arrived.at[pl.ds(0, others)]))

    mates = [(d, c) for d in reversed(range(groups)) for c in range(CORES) if d or c]

    def mate(d, c):
        return (partner(d), flipped(p, c, CORES))

    barrier = pltpu.get_barrier_semaphore()

    def greet(to):
        pl.semaphore_signal(barrier, inc=1, device_id=to, device_id_type=MESH)

    greeted = [0] * groups
    for mine in range(1, groups):
        for source, _, _ in sources(mine, length):
            greeted[source] += 1

        @pl.when(g == mine)
        def _():
            for source, _, _ in sources(mine, length):
                greet(at(source, p + mine))

    last_chip = p >= segs - CORES

    def of_last_chip(pos):
        return lax.rem(pos + segs, segs) >= segs - CORES

    for d in range(1, groups):
        @pl.when(jnp.logical_and(g != d, of_last_chip(p - d)))
        def _():
            greet(at(d, p - d))

    column = sorted({CORES * d for d in range(1, chips)} | {segs - d for d in range(1, groups)})
    for d in column:
        greet(at(g, p + d))
    for d, c in mates:
        greet(mate(d, c))

    small = [
        pltpu.make_async_copy(src, dst, in_sem.at[i])
        for i, (src, dst) in enumerate([
            (basis_hbm, own), (row_hbm, rows), (col_hbm, cols), (count_hbm, count),
            (prev_hbm, prev), (energies_hbm, energies), (beta_prev_hbm, beta_prev),
        ])
    ]
    for copy in small:
        copy.start()

    def tile_copy(i):
        some = pl.ds(i * step, step)
        return pltpu.make_async_copy(tiles_hbm.at[some], tiles.at[some], tile_sem.at[i])

    for i in range(slots // step):
        tile_copy(i).start()

    def stack(ref, out):
        for t in range(sides):
            high, low = split(ref[:, t * width : (t + 1) * width])
            out[t] = jnp.concatenate([high, low], axis=0)

    def multiply(picked, high, low, dims):
        both_parts = lax.dot_general(picked, high, dims, preferred_element_type=f32)
        both_parts += lax.dot_general(picked, low, dims, preferred_element_type=f32)
        return both_parts[:vectors] + both_parts[vectors:]

    def added(index, t):
        value = jnp.zeros((vectors, width), f32)
        for k in range(slots):
            live = jnp.logical_and(index[0, k] == t, k < count[0, 0])
            value = value + products[k] * jnp.where(live, 1.0, 0.0).astype(f32)
        return value

    def scatter(index, out, then=lambda d: None):
        whole = part // width
        for d in reversed(range(groups)):
            for t in range(whole):
                h = partner(d)
                out[h, :, t * width : (t + 1) * width] = added(index, h * whole + t)
            if whole:
                then(d)
        if not whole:
            for t in range(sides):
                value = added(index, t)
                for c in range(0, width, part):
                    out[(t * width + c) // part] = value[:, c : c + part]
            for d in reversed(range(groups)):
                then(d)

    def far_copy(to_group, i):
        _, first, lanes = sources(to_group, length)[i]
        lanes = slice(first, first + lanes)
        return post(FAR, own.at[:, lanes], far.at[:, lanes], at(to_group, p - to_group + segs))

    far_copies = [
        (source, to_group, i)
        for to_group in reversed(range(1, groups))
        for i, (source, _, _) in enumerate(sources(to_group, length))
    ]

    def backward():
        with jax.named_scope("ph_small"):
            for copy in small[1:4]:
                copy.wait()
        stack(own, own_split)

        def some(i, carry):
            tile_copy(i).wait()
            for j in range(step):
                k = i * step + j
                high, low = split(tiles[k])
                products[k] = multiply(own_split[rows[0, k]], high, low, NN)
            return carry

        with jax.named_scope("ph_bwd"):
            lax.fori_loop(0, slots // step, some, 0)
        scatter(cols, back)

    early = p < CORES
    small[0].wait()
    pl.when(early)(backward)
    with jax.named_scope("ph_barrier"):
        for mine in reversed(range(groups)):
            @pl.when(g == mine)
            def _():
                expected = greeted[mine] + len(column) + len(mates)
                for last in (False, True):
                    pl.when(last_chip == last)(
                        functools.partial(pl.semaphore_wait, barrier, expected + (others if last and mine else 0))
                    )
                for last in (True, False):
                    for source, to_group, i in far_copies:
                        if source == mine:
                            pl.when(of_last_chip(p - to_group) == last)(far_copy(to_group, i).start)
    for d in range(1, chips):
        pl.semaphore_signal(ready, inc=1, device_id=at(g, p + CORES * d), device_id_type=MESH)
    pl.when(jnp.logical_not(early))(backward)

    @pl.when(jnp.logical_not(last_chip))
    def _():
        for d in reversed(range(1, groups)):
            post(CROSS, back.at[partner(d)], relay.at[d], at(partner(d), p)).start()

    @pl.when(g == 0)
    def _():
        far[...] = own[...]

    with jax.named_scope("ph_pre"):
        for copy in small[4:]:
            copy.wait()
        lanes = pl.ds(pl.multiple_of(g * part, part), part)
        basis_part, prev_part = own[:, lanes], prev[:, lanes]
        weighted = energies[:, lanes] * basis_part
        both = jnp.concatenate([basis_part, weighted, prev_part], axis=0)
        inner = exact(both, basis_part, NT)
        inner = jnp.concatenate(
            [
                inner[: 2 * vectors],
                exact(beta_prev[...], inner[2 * vectors :], NN),
                jnp.zeros((vectors, vectors), f32),
            ],
            axis=0,
        )
        offset = weighted - exact(beta_prev[...], prev_part, NN)
        slot = g * CORES + core
        near[slot] = packed(inner)
    for d, c in mates:
        post(NEAR, near.at[slot], near.at[slot], mate(d, c)).start()

    @pl.when(last_chip)
    def _():
        for d in reversed(range(groups)):
            @pl.when(jnp.logical_or(g != 0, d != 0))
            def _():
                post(BACK, back.at[partner(d)], arrived.at[d], at(partner(d), p + g)).start()

        @pl.when(g == 0)
        def _():
            arrived[0] = back[0]

    pairs = 2 if slots % 2 == 0 else 1

    def turn(i, carry):
        for j in range(pairs):
            k = i * pairs + j
            highs[k], lows[k] = split(tiles[k].T)
        return carry

    with jax.named_scope("ph_turn"):
        lax.fori_loop(0, slots // pairs, turn, 0)

    def relay_on():
        with jax.named_scope("ph_cross"):
            landed(CROSS, relay.at[pl.ds(1, others)])
        for d in reversed(range(1, groups)):
            pl.when(g != d)(post(BACK, relay.at[d], arrived.at[d], at(g, p + partner(d))).start)
        pl.when(g != 0)(post(BACK, back.at[g], arrived.at[0], at(g, p + g)).start)
        for d in range(groups):
            @pl.when(g == d)
            def _():
                arrived[d] = relay[d] if d else back[0]

    pl.when(p < segs // 2)(relay_on)

    with jax.named_scope("ph_farwait"):
        pl.when(g != 0)(lambda: landed(FAR, far))

    stack(far, far_split)

    with jax.named_scope("ph_fwd"):
        for k in range(slots):
            products[k] = multiply(far_split[cols[0, k]], highs[k], lows[k], NN)
    with jax.named_scope("ph_scat2"):
        def pass_on(d):
            if d:
                post(FORTH, forth.at[partner(d)], arrived.at[groups + d - 1], at(partner(d), p)).start()

        scatter(rows, forth, pass_on)
    pl.when(jnp.logical_not(jnp.logical_or(p < segs // 2, last_chip)))(relay_on)

    def to_all(which, buffer, value):
        me = g * segs + p
        buffer[me] = value

        def copy(dg, dp):
            return post(which, buffer.at[me], buffer.at[me], (flipped(g, dg, groups), flipped(p, dp, segs)))

        if devices <= 64:
            apart = [
                (dp * CORES + c, dg)
                for dp in reversed(range(chips)) for dg in reversed(range(groups)) for c in range(CORES)
            ]
            apart.remove((0, 0))
            for dp, dg in apart:
                copy(dg, dp).start()
        else:
            def one(d, carry):
                copy(d // segs, lax.rem(d, segs)).start()
                return carry

            lax.fori_loop(1, devices, one, 0)

    def summed(buffer):
        value = buffer[0]
        for i in range(1, buffer.shape[0]):
            value = value + buffer[i]
        return value

    with jax.named_scope("ph_mid"):
        mid = jnp.zeros((vectors, vectors), f32)
        for h in range(groups):
            mid = mid + exact(back[h], far[:, h * part : (h + 1) * part], NT)
        mids[chip] = folded(mid + mid.T)
    for d in reversed(range(1, chips)):
        post(MIDS, mids.at[chip], mids.at[chip], at(g, p + CORES * d)).start()

    with jax.named_scope("ph_near"):
        landed(NEAR, near.at[pl.ds(0, groups * CORES - 1)])
        late[chip] = summed(near)
    for d in reversed(range(1, chips)):
        post(LATE, late.at[chip], late.at[chip], at(g, p + CORES * d)).start()

    with jax.named_scope("ph_kown"):
        pieces = split3(own[...])
        for i, (_, piece) in enumerate(TERMS):
            stack_ref[(2 * i + 1) * vectors : (2 * i + 2) * vectors, :] = pieces[piece]
    with jax.named_scope("ph_rswait"):
        settle_back()
        landed(FORTH, arrived.at[pl.ds(groups, others)])

    with jax.named_scope("ph_gram"):
        pl.semaphore_wait(ready, chips - 1)
        mine = forth[g] + offset
        for d in range(2 * groups - 1):
            mine = mine + arrived[d]
        rest[:, lanes] = mine
        value = folded(exact(mine, mine, NT))
        for d in reversed(range(1, groups)):
            post(GATHER, rest.at[:, lanes], rest.at[:, lanes], at(partner(d), p)).start()
        to_all(LASTS, lasts, value)

    with jax.named_scope("ph_latewait"):
        landed(LATE, late.at[pl.ds(0, chips - 1)])
    with jax.named_scope("ph_mids1"):
        landed(MIDS, mids.at[pl.ds(0, chips - 1)])
        ends[slot] = summed(mids)
    for d, c in mates:
        post(ENDS, ends.at[slot], ends.at[slot], mate(d, c)).start()
    with jax.named_scope("ph_gatherwait"):
        landed(GATHER, rest.at[:, pl.ds(0, others * part)])
    with jax.named_scope("ph_krest"):
        pieces = split3(rest[...])
        for i, (_, piece) in enumerate(TERMS):
            stack_ref[2 * i * vectors : (2 * i + 1) * vectors, :] = pieces[piece]
    with jax.named_scope("ph_sendwait"):
        for mine in range(groups):
            for last in (True, False):
                @pl.when(jnp.logical_and(g == mine, last_chip == last))
                def _():
                    all_gone(mine, last)
    with jax.named_scope("ph_midswait"):
        landed(ENDS, ends.at[pl.ds(0, groups * CORES - 1)])
    with jax.named_scope("ph_known"):
        inner = unpacked(summed(late))
        own_own, shift = inner[:vectors], inner[2 * vectors : 3 * vectors]
        applied_own = inner[vectors : 2 * vectors] + unfolded(summed(ends), vectors)
        rest_own, alpha_t = applied_own - shift, applied_own / total
        alpha_ref[...] = alpha_t
        row_at = lax.broadcasted_iota(jnp.int32, (vectors, vectors), 0)
        col_at = lax.broadcasted_iota(jnp.int32, (vectors, vectors), 1)
        identity = jnp.where(row_at == col_at, 1.0, 0.0).astype(f32)
        wide_ref[...] = jnp.concatenate([identity, -alpha_t] * len(TERMS), axis=1)
        known_ref[...] = (
            exact(exact(alpha_t, own_own, NN) - rest_own, alpha_t, NT) - exact(alpha_t, rest_own, NT)
        )
    with jax.named_scope("ph_lastswait"):
        landed(LASTS, lasts.at[pl.ds(0, devices - 1)])
    sums_ref[...] = summed(lasts)


def finish(
    total, sums_ref, alpha_t_ref, known_ref, wide_ref, stack_ref, next_hbm, alpha_hbm, beta_hbm,
    ahead, alpha, beta, sem,
):
    vectors, length = ahead.shape
    alpha[...] = alpha_t_ref[...].T
    outs = [pltpu.make_async_copy(alpha, alpha_hbm, sem.at[0]), pltpu.make_async_copy(beta, beta_hbm, sem.at[1])]
    outs[0].start()
    gram = (unfolded(sums_ref[...], vectors) + known_ref[...]) / total
    cuts = [slice(i, min(i + LANES, wide_ref.shape[1])) for i in range(0, wide_ref.shape[1], LANES)]
    with jax.named_scope("ph_factor"):
        upper, weights = factored(gram, [wide_ref[:, cut] for cut in cuts])
    left = []
    for cut, values in zip(cuts, weights, strict=True):
        pieces = split3(values)
        term = lax.broadcasted_iota(jnp.int32, values.shape, 1) // (2 * vectors) + cut.start // (2 * vectors)
        value = pieces[0].astype(f32)
        for i, (piece, _) in enumerate(TERMS):
            if piece:
                value = jnp.where(term == i, pieces[piece].astype(f32), value)
        left.append(value.astype(bf16))
    left = jnp.concatenate(left, axis=1)
    with jax.named_scope("ph_last"):
        half = length // 2
        for i in range(2):
            lanes = slice(i * half, (i + 1) * half)
            ahead[:, lanes] = lax.dot_general(left, stack_ref[:, lanes], NN, preferred_element_type=f32)
            outs.append(pltpu.make_async_copy(ahead.at[:, lanes], next_hbm.at[:, lanes], sem.at[2 + i]))
            outs[-1].start()
            if i == 0:
                beta[...] = upper.T
                outs[1].start()
    for copy in outs:
        copy.wait()


def shards(groups, segs, tiles, tile_row, tile_col, tile_count, energies, basis, prev_basis, beta_prev):
    slots, width = tiles.shape[2], tiles.shape[-1]
    vectors, length = basis.shape
    sides, part, chips = length // width, length // groups, segs // CORES
    step = next(n for n in (4, 3, 2, 1) if slots % n == 0)
    total = float(length * segs)
    dma = pltpu.SemaphoreType.DMA
    block, square = (vectors, length), (vectors, vectors)
    message, fold = (vectors // 2, 8 * vectors), (vectors * vectors // LANES, LANES)
    kib = max(
        sent_kib(groups, segs, vectors, length, mine, last)
        for mine in range(groups) for last in (True, False)
    )
    vmem = pl.BlockSpec(memory_space=pltpu.VMEM)
    stack, alpha_t, known, wide, sums = pl.pallas_call(
        functools.partial(kernel, groups, segs, total),
        out_shape=(
            pltpu.VMEM((2 * len(TERMS) * vectors, length), bf16),
            pltpu.VMEM(square, f32),
            pltpu.VMEM(square, f32),
            pltpu.VMEM((vectors, 2 * len(TERMS) * vectors), f32),
            pltpu.VMEM(fold, f32),
        ),
        in_specs=[pl.BlockSpec(memory_space=pltpu.HBM)] * 8,
        out_specs=(vmem,) * 5,
        scratch_shapes=[
            pltpu.VMEM((slots, width, width), f32),
            pltpu.VMEM((slots, width, width), bf16),
            pltpu.VMEM((slots, width, width), bf16),
            pltpu.SMEM((1, slots), jnp.int32),
            pltpu.SMEM((1, slots), jnp.int32),
            pltpu.SMEM((1, 1), jnp.int32),
            pltpu.VMEM((1, length), f32),
            pltpu.VMEM(block, f32),
            pltpu.VMEM(block, f32),
            pltpu.VMEM(block, f32),
            pltpu.VMEM(square, f32),
            pltpu.VMEM((sides, 2 * vectors, width), bf16),
            pltpu.VMEM((sides, 2 * vectors, width), bf16),
            pltpu.VMEM((slots, vectors, width), f32),
            pltpu.VMEM((groups, vectors, part), f32),
            pltpu.VMEM((groups, vectors, part), f32),
            pltpu.VMEM((groups, vectors, part), f32),
            pltpu.VMEM((2 * groups - 1, vectors, part), f32),
            pltpu.VMEM(block, f32),
            pltpu.VMEM((groups * CORES, *message), f32),
            pltpu.VMEM((chips, *message), f32),
            pltpu.VMEM((chips, *fold), f32),
            pltpu.VMEM((groups * CORES, *fold), f32),
            pltpu.VMEM((groups * segs, *fold), f32),
            pltpu.VMEM((kib, *fold), f32),
            dma((7,)), dma((slots // step,)), dma, dma((10,)),
            pltpu.SemaphoreType.REGULAR,
        ],
        compiler_params=pltpu.CompilerParams(collective_id=0, has_side_effects=True),
    )(
        tiles.reshape(slots, width, width),
        tile_row.reshape(1, slots),
        tile_col.reshape(1, slots),
        tile_count.reshape(1, 1),
        energies.reshape(1, length),
        basis,
        prev_basis,
        beta_prev,
    )
    held = [pltpu.with_memory_space_constraint(x, pltpu.VMEM) for x in (sums, alpha_t, known, wide, stack)]
    return pl.pallas_call(
        functools.partial(finish, total),
        out_shape=(
            jax.ShapeDtypeStruct(block, f32),
            jax.ShapeDtypeStruct(square, f32),
            jax.ShapeDtypeStruct(square, f32),
        ),
        in_specs=[vmem] * 5,
        out_specs=(pl.BlockSpec(memory_space=pltpu.HBM),) * 3,
        scratch_shapes=[pltpu.VMEM(block, f32), pltpu.VMEM(square, f32), pltpu.VMEM(square, f32), dma((4,))],
    )(*held)


def solution(mesh):
    groups, segs = mesh.shape["grp"], mesh.shape["pos"]
    in_specs = (
        P("grp", "pos", None, None, None),
        P("grp", "pos", None),
        P("grp", "pos", None),
        P("grp", "pos"),
        P("pos"),
        P(None, "pos"),
        P(None, "pos"),
        P(),
    )
    out_specs = (P(None, "pos"), P(), P())
    return jax.shard_map(
        functools.partial(shards, groups, segs),
        mesh=mesh, in_specs=in_specs, out_specs=out_specs, check_vma=False,
    )
```

```python
import functools

import jax
import jax.numpy as jnp
from jax import lax
from jax.experimental import pallas as pl
from jax.experimental.pallas import tpu as pltpu
from jax.sharding import PartitionSpec as P

MESH = pl.DeviceIdType.MESH
NT = (((1,), (1,)), ((), ()))
NN = (((1,), (0,)), ((), ()))
f32 = jnp.float32
bf16 = jnp.bfloat16
CORES = 2
LANES = 128
TERMS = ((0, 0), (0, 1), (1, 0), (0, 2), (2, 0), (1, 1))


def exact(left, right, dims):
    return lax.dot_general(
        left, right, dims, precision=lax.Precision.HIGHEST, preferred_element_type=f32
    )


def split(values):
    high = values.astype(bf16)
    return high, (values - high.astype(f32)).astype(bf16)


def split3(values):
    high = values.astype(bf16)
    rest = values - high.astype(f32)
    middle = rest.astype(bf16)
    return high, middle, (rest - middle.astype(f32)).astype(bf16)


def packed(values):
    rows = values.shape[0] // 8
    return jnp.concatenate([values[i * rows : (i + 1) * rows] for i in range(8)], axis=1)


def unpacked(values):
    lanes = values.shape[1] // 8
    return jnp.concatenate([values[:, i * lanes : (i + 1) * lanes] for i in range(8)], axis=0)


def folded(values):
    rows = values.size // LANES
    return jnp.concatenate([values[i : i + rows] for i in range(0, values.shape[0], rows)], axis=1)


def unfolded(values, lanes):
    return jnp.concatenate([values[:, i : i + lanes] for i in range(0, LANES, lanes)], axis=0)


def sources(group, length):
    half, quarter = length // 2, length // 4
    low, high = group & (group - 1), group - (1 << (group.bit_length() - 1))
    if low == high:
        own = half + quarter if group == 1 else half
        return [(group, 0, own), (low, own, length - own)]
    return [(group, 0, half), (low, half, quarter), (high, half + quarter, quarter)]


def factored(gram, wide):
    n = gram.shape[0]
    wide = [*wide, gram]
    row_at = lax.broadcasted_iota(jnp.int32, (n, 1), 0)
    columns = [jnp.broadcast_to(gram[:, k : k + 1], (n, LANES)) for k in range(n)]
    done = [jnp.zeros(x.shape, f32) for x in wide]
    for j in range(n):
        corner = columns[j][j : j + 1]
        inverse, root = 1.0 / corner, lax.rsqrt(corner)
        for i, x in enumerate(wide):
            lanes = x.shape[1]
            row = x[j : j + 1]
            done[i] = jnp.where(row_at == j, row * root[:, :lanes], done[i])
            wide[i] = x - columns[j][:, :lanes] * (row * inverse[:, :lanes])
        for k in range(j + 1, n):
            columns[k] = columns[k] - columns[j] * (columns[k][j : j + 1] * inverse)
    return done[-1], done[:-1]


def flipped(value, d, count):
    out, bit = value, 1
    while bit < count:
        if not isinstance(d, int) or d & bit:
            out = out + (d // bit % 2) * (bit - 2 * bit * lax.rem(value // bit, 2))
        bit *= 2
    return out


def sent_kib(groups, segs, vectors, length, mine, last):
    others, block = groups - 1, vectors * length // groups // 256
    lanes = sum(
        n for to_group in range(1, groups)
        for source, _, n in sources(to_group, length) if source == mine
    )
    blocks = (0 if last else others) + (groups if last and mine else others) + 2 * others
    messages = groups * CORES - 1 + segs // CORES - 1
    return (
        lanes * vectors // 256 + blocks * block
        + (messages * 5 * vectors + (groups * segs - 1) * vectors) * vectors // 256
    )


def kernel(
    groups, segs, total,
    tiles_hbm, row_hbm, col_hbm, count_hbm, energies_hbm, basis_hbm, prev_hbm, beta_prev_hbm,
    stack_ref, alpha_ref, known_ref, wide_ref, sums_ref,
    tiles, highs, lows, rows, cols, count, energies, own, far, prev, beta_prev,
    own_split, far_split, products, back, relay, forth, arrived, rest, near, late, mids, ends, lasts,
    bulk, in_sem, tile_sem, sent, came, ready,
):
    g, p = lax.axis_index("grp"), lax.axis_index("pos")
    slots, width = tiles.shape[0], tiles.shape[-1]
    vectors, length = own.shape
    sides = length // width
    part = length // groups
    chips, devices = segs // CORES, groups * segs
    core, chip = lax.rem(p, CORES), p // CORES
    step = slots // tile_sem.shape[0]
    others = groups - 1
    FAR, CROSS, BACK, FORTH, GATHER, NEAR, LATE, MIDS, ENDS, LASTS = range(10)

    def at(group, pos):
        return (group, lax.rem(pos + segs, segs))

    def partner(d):
        return flipped(g, d, groups)

    def send(src, dst, send_sem, recv_sem, to):
        return pltpu.make_async_remote_copy(
            src_ref=src, dst_ref=dst, send_sem=send_sem, recv_sem=recv_sem,
            device_id=to, device_id_type=MESH,
        )

    def post(which, src, dst, to):
        return send(src, dst, sent, came.at[which], to)

    def landed(which, ref):
        pltpu.make_async_copy(ref, ref, came.at[which]).wait()

    def all_gone(mine, last):
        ref = bulk.at[pl.ds(0, sent_kib(groups, segs, vectors, length, mine, last))]
        pltpu.make_async_copy(ref, ref, sent).wait()

    def settle_back():
        whole = jnp.logical_and(p >= segs - CORES, g != 0)
        pl.when(whole)(lambda: landed(BACK, arrived.at[pl.ds(0, groups)]))
        pl.when(jnp.logical_not(whole))(lambda: landed(BACK, arrived.at[pl.ds(0, others)]))

    mates = [(d, c) for d in reversed(range(groups)) for c in range(CORES) if d or c]

    def mate(d, c):
        return (partner(d), flipped(p, c, CORES))

    barrier = pltpu.get_barrier_semaphore()

    def greet(to):
        pl.semaphore_signal(barrier, inc=1, device_id=to, device_id_type=MESH)

    greeted = [0] * groups
    for mine in range(1, groups):
        for source, _, _ in sources(mine, length):
            greeted[source] += 1

        @pl.when(g == mine)
        def _():
            for source, _, _ in sources(mine, length):
                greet(at(source, p + mine))

    last_chip = p >= segs - CORES

    def of_last_chip(pos):
        return lax.rem(pos + segs, segs) >= segs - CORES

    for d in range(1, groups):
        @pl.when(jnp.logical_and(g != d, of_last_chip(p - d)))
        def _():
            greet(at(d, p - d))

    column = sorted({CORES * d for d in range(1, chips)} | {segs - d for d in range(1, groups)})
    for d in column:
        greet(at(g, p + d))
    for d, c in mates:
        greet(mate(d, c))

    small = [
        pltpu.make_async_copy(src, dst, in_sem.at[i])
        for i, (src, dst) in enumerate([
            (basis_hbm, own), (row_hbm, rows), (col_hbm, cols), (count_hbm, count),
            (prev_hbm, prev), (energies_hbm, energies), (beta_prev_hbm, beta_prev),
        ])
    ]
    for copy in small:
        copy.start()

    def tile_copy(i):
        some = pl.ds(i * step, step)
        return pltpu.make_async_copy(tiles_hbm.at[some], tiles.at[some], tile_sem.at[i])

    for i in range(slots // step):
        tile_copy(i).start()

    def stack(ref, out):
        for t in range(sides):
            high, low = split(ref[:, t * width : (t + 1) * width])
            out[t] = jnp.concatenate([high, low], axis=0)

    def multiply(picked, high, low, dims):
        both_parts = lax.dot_general(picked, high, dims, preferred_element_type=f32)
        both_parts += lax.dot_general(picked, low, dims, preferred_element_type=f32)
        return both_parts[:vectors] + both_parts[vectors:]

    def added(index, t):
        value = jnp.zeros((vectors, width), f32)
        for k in range(slots):
            live = jnp.logical_and(index[0, k] == t, k < count[0, 0])
            value = value + products[k] * jnp.where(live, 1.0, 0.0).astype(f32)
        return value

    def scatter(index, out, then=lambda d: None):
        whole = part // width
        for d in reversed(range(groups)):
            for t in range(whole):
                h = partner(d)
                out[h, :, t * width : (t + 1) * width] = added(index, h * whole + t)
            if whole:
                then(d)
        if not whole:
            for t in range(sides):
                value = added(index, t)
                for c in range(0, width, part):
                    out[(t * width + c) // part] = value[:, c : c + part]
            for d in reversed(range(groups)):
                then(d)

    def far_copy(to_group, i):
        _, first, lanes = sources(to_group, length)[i]
        lanes = slice(first, first + lanes)
        return post(FAR, own.at[:, lanes], far.at[:, lanes], at(to_group, p - to_group + segs))

    far_copies = [
        (source, to_group, i)
        for to_group in reversed(range(1, groups))
        for i, (source, _, _) in enumerate(sources(to_group, length))
    ]

    def backward():
        with jax.named_scope("ph_small"):
            for copy in small[1:4]:
                copy.wait()
        stack(own, own_split)

        def some(i, carry):
            tile_copy(i).wait()
            for j in range(step):
                k = i * step + j
                high, low = split(tiles[k])
                products[k] = multiply(own_split[rows[0, k]], high, low, NN)
            return carry

        with jax.named_scope("ph_bwd"):
            lax.fori_loop(0, slots // step, some, 0)
        scatter(cols, back)

    early = p < CORES
    small[0].wait()
    pl.when(early)(backward)
    with jax.named_scope("ph_barrier"):
        for mine in reversed(range(groups)):
            @pl.when(g == mine)
            def _():
                expected = greeted[mine] + len(column) + len(mates)
                for last in (False, True):
                    pl.when(last_chip == last)(
                        functools.partial(pl.semaphore_wait, barrier, expected + (others if last and mine else 0))
                    )
                for last in (True, False):
                    for source, to_group, i in far_copies:
                        if source == mine:
                            pl.when(of_last_chip(p - to_group) == last)(far_copy(to_group, i).start)
    for d in range(1, chips):
        pl.semaphore_signal(ready, inc=1, device_id=at(g, p + CORES * d), device_id_type=MESH)
    pl.when(jnp.logical_not(early))(backward)

    @pl.when(jnp.logical_not(last_chip))
    def _():
        for d in reversed(range(1, groups)):
            post(CROSS, back.at[partner(d)], relay.at[d], at(partner(d), p)).start()

    @pl.when(g == 0)
    def _():
        far[...] = own[...]

    with jax.named_scope("ph_pre"):
        for copy in small[4:]:
            copy.wait()
        lanes = pl.ds(pl.multiple_of(g * part, part), part)
        basis_part, prev_part = own[:, lanes], prev[:, lanes]
        weighted = energies[:, lanes] * basis_part
        both = jnp.concatenate([basis_part, weighted, prev_part], axis=0)
        inner = exact(both, basis_part, NT)
        inner = jnp.concatenate(
            [
                inner[: 2 * vectors],
                exact(beta_prev[...], inner[2 * vectors :], NN),
                jnp.zeros((vectors, vectors), f32),
            ],
            axis=0,
        )
        offset = weighted - exact(beta_prev[...], prev_part, NN)
        slot = g * CORES + core
        near[slot] = packed(inner)
    for d, c in mates:
        post(NEAR, near.at[slot], near.at[slot], mate(d, c)).start()

    @pl.when(last_chip)
    def _():
        for d in reversed(range(groups)):
            @pl.when(jnp.logical_or(g != 0, d != 0))
            def _():
                post(BACK, back.at[partner(d)], arrived.at[d], at(partner(d), p + g)).start()

        @pl.when(g == 0)
        def _():
            arrived[0] = back[0]

    pairs = 2 if slots % 2 == 0 else 1

    def turn(i, carry):
        for j in range(pairs):
            k = i * pairs + j
            highs[k], lows[k] = split(tiles[k].T)
        return carry

    with jax.named_scope("ph_turn"):
        lax.fori_loop(0, slots // pairs, turn, 0)

    def relay_on():
        with jax.named_scope("ph_cross"):
            landed(CROSS, relay.at[pl.ds(1, others)])
        for d in reversed(range(1, groups)):
            pl.when(g != d)(post(BACK, relay.at[d], arrived.at[d], at(g, p + partner(d))).start)
        pl.when(g != 0)(post(BACK, back.at[g], arrived.at[0], at(g, p + g)).start)
        for d in range(groups):
            @pl.when(g == d)
            def _():
                arrived[d] = relay[d] if d else back[0]

    pl.when(p < segs // 2)(relay_on)

    with jax.named_scope("ph_farwait"):
        pl.when(g != 0)(lambda: landed(FAR, far))

    stack(far, far_split)

    with jax.named_scope("ph_fwd"):
        for k in range(slots):
            products[k] = multiply(far_split[cols[0, k]], highs[k], lows[k], NN)
    with jax.named_scope("ph_scat2"):
        def pass_on(d):
            if d:
                post(FORTH, forth.at[partner(d)], arrived.at[groups + d - 1], at(partner(d), p)).start()

        scatter(rows, forth, pass_on)
    pl.when(jnp.logical_not(jnp.logical_or(p < segs // 2, last_chip)))(relay_on)

    def to_all(which, buffer, value):
        me = g * segs + p
        buffer[me] = value

        def copy(dg, dp):
            return post(which, buffer.at[me], buffer.at[me], (flipped(g, dg, groups), flipped(p, dp, segs)))

        if devices <= 64:
            apart = [
                (dp * CORES + c, dg)
                for dp in reversed(range(chips)) for dg in reversed(range(groups)) for c in range(CORES)
            ]
            apart.remove((0, 0))
            for dp, dg in apart:
                copy(dg, dp).start()
        else:
            def one(d, carry):
                copy(d // segs, lax.rem(d, segs)).start()
                return carry

            lax.fori_loop(1, devices, one, 0)

    def summed(buffer):
        value = buffer[0]
        for i in range(1, buffer.shape[0]):
            value = value + buffer[i]
        return value

    with jax.named_scope("ph_mid"):
        mid = jnp.zeros((vectors, vectors), f32)
        for h in range(groups):
            mid = mid + exact(back[h], far[:, h * part : (h + 1) * part], NT)
        mids[chip] = folded(mid + mid.T)
    for d in reversed(range(1, chips)):
        post(MIDS, mids.at[chip], mids.at[chip], at(g, p + CORES * d)).start()

    with jax.named_scope("ph_near"):
        landed(NEAR, near.at[pl.ds(0, groups * CORES - 1)])
        late[chip] = summed(near)
    for d in reversed(range(1, chips)):
        post(LATE, late.at[chip], late.at[chip], at(g, p + CORES * d)).start()

    with jax.named_scope("ph_kown"):
        pieces = split3(own[...])
        for i, (_, piece) in enumerate(TERMS):
            stack_ref[(2 * i + 1) * vectors : (2 * i + 2) * vectors, :] = pieces[piece]
    with jax.named_scope("ph_rswait"):
        settle_back()
        landed(FORTH, arrived.at[pl.ds(groups, others)])

    with jax.named_scope("ph_gram"):
        pl.semaphore_wait(ready, chips - 1)
        mine = forth[g] + offset
        for d in range(2 * groups - 1):
            mine = mine + arrived[d]
        value = folded(exact(mine, mine, NT))
        to_all(LASTS, lasts, value)
        rest[:, lanes] = mine
        for d in reversed(range(1, groups)):
            post(GATHER, rest.at[:, lanes], rest.at[:, lanes], at(partner(d), p)).start()

    with jax.named_scope("ph_latewait"):
        landed(LATE, late.at[pl.ds(0, chips - 1)])
    with jax.named_scope("ph_mids1"):
        landed(MIDS, mids.at[pl.ds(0, chips - 1)])
        ends[slot] = summed(mids)
    for d, c in mates:
        post(ENDS, ends.at[slot], ends.at[slot], mate(d, c)).start()
    with jax.named_scope("ph_gatherwait"):
        landed(GATHER, rest.at[:, pl.ds(0, others * part)])
    with jax.named_scope("ph_krest"):
        pieces = split3(rest[...])
        for i, (_, piece) in enumerate(TERMS):
            stack_ref[2 * i * vectors : (2 * i + 1) * vectors, :] = pieces[piece]
    with jax.named_scope("ph_sendwait"):
        for mine in range(groups):
            for last in (True, False):
                @pl.when(jnp.logical_and(g == mine, last_chip == last))
                def _():
                    all_gone(mine, last)
    with jax.named_scope("ph_midswait"):
        landed(ENDS, ends.at[pl.ds(0, groups * CORES - 1)])
    with jax.named_scope("ph_known"):
        inner = unpacked(summed(late))
        own_own, shift = inner[:vectors], inner[2 * vectors : 3 * vectors]
        applied_own = inner[vectors : 2 * vectors] + unfolded(summed(ends), vectors)
        rest_own, alpha_t = applied_own - shift, applied_own / total
        alpha_ref[...] = alpha_t
        row_at = lax.broadcasted_iota(jnp.int32, (vectors, vectors), 0)
        col_at = lax.broadcasted_iota(jnp.int32, (vectors, vectors), 1)
        identity = jnp.where(row_at == col_at, 1.0, 0.0).astype(f32)
        wide_ref[...] = jnp.concatenate([identity, -alpha_t] * len(TERMS), axis=1)
        known_ref[...] = (
            exact(exact(alpha_t, own_own, NN) - rest_own, alpha_t, NT) - exact(alpha_t, rest_own, NT)
        )
    with jax.named_scope("ph_lastswait"):
        landed(LASTS, lasts.at[pl.ds(0, devices - 1)])
    sums_ref[...] = summed(lasts)


def finish(
    total, sums_ref, alpha_t_ref, known_ref, wide_ref, stack_ref, next_hbm, alpha_hbm, beta_hbm,
    ahead, alpha, beta, sem,
):
    vectors, length = ahead.shape
    alpha[...] = alpha_t_ref[...].T
    outs = [pltpu.make_async_copy(alpha, alpha_hbm, sem.at[0]), pltpu.make_async_copy(beta, beta_hbm, sem.at[1])]
    outs[0].start()
    gram = (unfolded(sums_ref[...], vectors) + known_ref[...]) / total
    cuts = [slice(i, min(i + LANES, wide_ref.shape[1])) for i in range(0, wide_ref.shape[1], LANES)]
    with jax.named_scope("ph_factor"):
        upper, weights = factored(gram, [wide_ref[:, cut] for cut in cuts])
    left = []
    for cut, values in zip(cuts, weights, strict=True):
        pieces = split3(values)
        term = lax.broadcasted_iota(jnp.int32, values.shape, 1) // (2 * vectors) + cut.start // (2 * vectors)
        value = pieces[0].astype(f32)
        for i, (piece, _) in enumerate(TERMS):
            if piece:
                value = jnp.where(term == i, pieces[piece].astype(f32), value)
        left.append(value.astype(bf16))
    left = jnp.concatenate(left, axis=1)
    with jax.named_scope("ph_last"):
        half = length // 2
        for i in range(2):
            lanes = slice(i * half, (i + 1) * half)
            ahead[:, lanes] = lax.dot_general(left, stack_ref[:, lanes], NN, preferred_element_type=f32)
            outs.append(pltpu.make_async_copy(ahead.at[:, lanes], next_hbm.at[:, lanes], sem.at[2 + i]))
            outs[-1].start()
            if i == 0:
                beta[...] = upper.T
                outs[1].start()
    for copy in outs:
        copy.wait()


def shards(groups, segs, tiles, tile_row, tile_col, tile_count, energies, basis, prev_basis, beta_prev):
    slots, width = tiles.shape[2], tiles.shape[-1]
    vectors, length = basis.shape
    sides, part, chips = length // width, length // groups, segs // CORES
    step = next(n for n in (4, 3, 2, 1) if slots % n == 0)
    total = float(length * segs)
    dma = pltpu.SemaphoreType.DMA
    block, square = (vectors, length), (vectors, vectors)
    message, fold = (vectors // 2, 8 * vectors), (vectors * vectors // LANES, LANES)
    kib = max(
        sent_kib(groups, segs, vectors, length, mine, last)
        for mine in range(groups) for last in (True, False)
    )
    vmem = pl.BlockSpec(memory_space=pltpu.VMEM)
    stack, alpha_t, known, wide, sums = pl.pallas_call(
        functools.partial(kernel, groups, segs, total),
        out_shape=(
            pltpu.VMEM((2 * len(TERMS) * vectors, length), bf16),
            pltpu.VMEM(square, f32),
            pltpu.VMEM(square, f32),
            pltpu.VMEM((vectors, 2 * len(TERMS) * vectors), f32),
            pltpu.VMEM(fold, f32),
        ),
        in_specs=[pl.BlockSpec(memory_space=pltpu.HBM)] * 8,
        out_specs=(vmem,) * 5,
        scratch_shapes=[
            pltpu.VMEM((slots, width, width), f32),
            pltpu.VMEM((slots, width, width), bf16),
            pltpu.VMEM((slots, width, width), bf16),
            pltpu.SMEM((1, slots), jnp.int32),
            pltpu.SMEM((1, slots), jnp.int32),
            pltpu.SMEM((1, 1), jnp.int32),
            pltpu.VMEM((1, length), f32),
            pltpu.VMEM(block, f32),
            pltpu.VMEM(block, f32),
            pltpu.VMEM(block, f32),
            pltpu.VMEM(square, f32),
            pltpu.VMEM((sides, 2 * vectors, width), bf16),
            pltpu.VMEM((sides, 2 * vectors, width), bf16),
            pltpu.VMEM((slots, vectors, width), f32),
            pltpu.VMEM((groups, vectors, part), f32),
            pltpu.VMEM((groups, vectors, part), f32),
            pltpu.VMEM((groups, vectors, part), f32),
            pltpu.VMEM((2 * groups - 1, vectors, part), f32),
            pltpu.VMEM(block, f32),
            pltpu.VMEM((groups * CORES, *message), f32),
            pltpu.VMEM((chips, *message), f32),
            pltpu.VMEM((chips, *fold), f32),
            pltpu.VMEM((groups * CORES, *fold), f32),
            pltpu.VMEM((groups * segs, *fold), f32),
            pltpu.VMEM((kib, *fold), f32),
            dma((7,)), dma((slots // step,)), dma, dma((10,)),
            pltpu.SemaphoreType.REGULAR,
        ],
        compiler_params=pltpu.CompilerParams(collective_id=0, has_side_effects=True),
    )(
        tiles.reshape(slots, width, width),
        tile_row.reshape(1, slots),
        tile_col.reshape(1, slots),
        tile_count.reshape(1, 1),
        energies.reshape(1, length),
        basis,
        prev_basis,
        beta_prev,
    )
    held = [pltpu.with_memory_space_constraint(x, pltpu.VMEM) for x in (sums, alpha_t, known, wide, stack)]
    return pl.pallas_call(
        functools.partial(finish, total),
        out_shape=(
            jax.ShapeDtypeStruct(block, f32),
            jax.ShapeDtypeStruct(square, f32),
            jax.ShapeDtypeStruct(square, f32),
        ),
        in_specs=[vmem] * 5,
        out_specs=(pl.BlockSpec(memory_space=pltpu.HBM),) * 3,
        scratch_shapes=[pltpu.VMEM(block, f32), pltpu.VMEM(square, f32), pltpu.VMEM(square, f32), dma((4,))],
    )(*held)


def solution(mesh):
    groups, segs = mesh.shape["grp"], mesh.shape["pos"]
    in_specs = (
        P("grp", "pos", None, None, None),
        P("grp", "pos", None),
        P("grp", "pos", None),
        P("grp", "pos"),
        P("pos"),
        P(None, "pos"),
        P(None, "pos"),
        P(),
    )
    out_specs = (P(None, "pos"), P(), P())
    return jax.shard_map(
        functools.partial(shards, groups, segs),
        mesh=mesh, in_specs=in_specs, out_specs=out_specs, check_vma=False,
    )
```
